128 devices in a mesh: sx: 8 (over y_hi, x), sy: 8 (over z, core), par: 2 (over y_lo).
Axes of the slice: x: 4, y: 4 (y_hi: 2, y_lo: 2; y = y_hi * 2 + y_lo), z: 4, core: 2. Of those that a mesh axis runs over, the one named last changes fastest.
Arguments:
- initial_state: float32 [64, 128, 128, 128], P('par', 'sx', 'sy'), may hold values from -6 to 6
- conductivity: float32 [64, 128, 128, 128], P('par', 'sx', 'sy'), may hold values from 0.1 to 1
- omega: bfloat16 [64, 64], replicated, may hold values from -0.75 to 0.75
- psi: bfloat16 [64, 128, 128, 128], P(None, 'sx', 'sy'), may hold values from -0.01171875 to 0.01171875
- range_prev: bfloat16 [64, 128, 128, 128], P('par', 'sx', 'sy'), may hold values from -3 to 3
- corange_prev: float32 [64, 64], P(None, 'par'), may hold values from -3 to 3
Outputs:
- final_state: float32 [64, 128, 128, 128], P('par', 'sx', 'sy')
- range_sketch: bfloat16 [64, 128, 128, 128], P('par', 'sx', 'sy')
- corange_sketch: float32 [64, 64], P(None, 'par')
The draws below stay inside these ranges and needn't reach their ends.
All inputs are finite; a program needn't handle non-finite values.
Results may differ from the reference program's by a relative error of at most 0.0033.
Values may be sent and summed in bfloat16 or wider, within the bound.
A program may use at most 192 MiB of HBM per device.

```python
import math
import jax
import jax.numpy as jnp

CX = 16
CY = 16
NZ = 128
R = 64
STEPS = 4
NX = 128
NY = 128
S = 64


def steps_of(stream_key, shape, cuts, least, top_value):
    def one(position, blocks):
        steps = jax.random.uniform(jax.random.fold_in(jax.random.fold_in(stream_key, 6), position), (blocks,), jnp.float32, least / len(cuts), top_value / len(cuts))
        return jnp.repeat(jnp.exp(steps), shape[position] // blocks).reshape((-1,) + (1,) * (len(shape) - position - 1))

    gain = one(*cuts[0])
    for cut in cuts[1:]:
        gain = gain * one(*cut)
    return gain


def centred(rng, extent, width, most, split=(), held_as=jnp.bfloat16):
    values = jax.random.normal(rng, extent, jnp.float32) * width
    if len(split) > 0:
        values = steps_of(rng, extent, split, -0.22, 0.18) * values
    return jnp.clip(values, min=-most, max=most).astype(held_as)


def setup_inputs(seed: int = 0) -> dict:
    streams_of = jax.random.split(jax.random.key(seed), 7)
    initial_state = centred(streams_of[0], (S, NX, NY, NZ), 1.0, 6.0, ((0, 2), (1, 8), (2, 8)), jnp.float32)
    conductivity = jnp.clip(jnp.exp(math.log(1.0) - 2.3025851 * jax.random.uniform(streams_of[1], (S, NX, NY, NZ), jnp.float32) ** steps_of(streams_of[1], (S, NX, NY, NZ), ((0, 2), (1, 8), (2, 8)), -0.2, 0.2)), 0.1, 1.0)
    omega = centred(streams_of[2], (S, R), S ** -0.5, 0.75)
    psi = centred(streams_of[3], (R, NX, NY, NZ), (8 * CX * CY * NZ) ** -0.5, 0.01171875, ((1, 8), (2, 8)))
    range_prev = centred(streams_of[4], (R, NX, NY, NZ), 0.5, 3.0, ((0, 2), (1, 8), (2, 8)))
    corange_prev = centred(streams_of[5], (R, S), 0.5, 3.0, ((1, 2),), jnp.float32)
    return {"initial_state": initial_state, "conductivity": conductivity, "omega": omega, "psi": psi, "range_prev": range_prev, "corange_prev": corange_prev}


def advance(state, conduct):
    field = jnp.pad(state, ((0, 0), (1, 1), (1, 1), (1, 1)))
    kpad = jnp.pad(conduct, ((0, 0), (1, 1), (1, 1), (1, 1)))
    center = field[:, 1:-1, 1:-1, 1:-1]
    kcen = kpad[:, 1:-1, 1:-1, 1:-1]
    shifts = [(2, 1, 1), (0, 1, 1), (1, 2, 1), (1, 0, 1), (1, 1, 2), (1, 1, 0)]
    total = jnp.zeros_like(center)
    for a, b, c in shifts:
        unb = field[:, a:a + center.shape[1], b:b + center.shape[2], c:c + center.shape[3]]
        knb = kpad[:, a:a + center.shape[1], b:b + center.shape[2], c:c + center.shape[3]]
        total = total + 0.5 * (kcen + knb) * (unb - center)
    return center + 0.16 * total


def reference(initial_state, conductivity, omega, psi, range_prev, corange_prev):
    state = initial_state
    for step in range(STEPS):
        state = advance(state, conductivity)
    snapshot = state.astype(jnp.bfloat16).astype(jnp.float32)
    range_new = jnp.einsum("sxyz,sr->rxyz", snapshot, omega.astype(jnp.float32))
    range_sketch = (range_prev.astype(jnp.float32) + range_new).astype(jnp.bfloat16)
    corange_new = jnp.einsum("rxyz,sxyz->rs", psi.astype(jnp.float32), snapshot)
    corange_sketch = corange_prev + corange_new
    return state, range_sketch, corange_sketch
```

```python
import functools

import jax
import jax.numpy as jnp
from jax import lax
from jax.experimental import pallas as pl
from jax.experimental.pallas import tpu as pltpu
from jax.sharding import PartitionSpec as P

STEPS = 4
H = STEPS
MESH = pl.DeviceIdType.MESH
F32 = jnp.float32
BF16 = jnp.bfloat16
CHUNK = 2


def kernel(
    u_hbm, k_hbm, omega_ref, psi_hbm, prev_hbm, cprev_ref,
    fin_hbm, range_hbm, cor_ref,
    u_in, k_in, xs, xr, ys, yr, snap, peer, psi, prev, acc, w_ref, red, part, gat1, part2, gat2,
    ua, ub, kk, cx, cy, cz, dd, rout,
    load_sem, aux_sem, xs_sem, xr_sem, ys_sem, yr_sem, ps_sem, pr_sem, fo_sem, ro_sem,
    a1s_sem, a1r_sem, a2s_sem, a2r_sem,
):
    S, X, Y, Z = u_in.shape
    NC = S // CHUNK
    XE = X + 2 * H
    R = psi.shape[0]
    RD = prev.shape[0]
    sx, sy, par = lax.axis_index("sx"), lax.axis_index("sy"), lax.axis_index("par")
    nsx, nsy = gat1.shape[0], gat2.shape[0]
    has = {("sx", 0): sx > 0, ("sx", 1): sx < nsx - 1, ("sy", 0): sy > 0, ("sy", 1): sy < nsy - 1}
    pos = {"sx": sx, "sy": sy}

    def chunk(c):
        return pl.ds(c * CHUNK, CHUNK)

    def load(c):
        return (
            pltpu.make_async_copy(u_hbm.at[chunk(c)], u_in.at[chunk(c)], load_sem.at[0, c]),
            pltpu.make_async_copy(k_hbm.at[chunk(c)], k_in.at[chunk(c)], load_sem.at[1, c]),
        )

    def halo(axis, side, c):
        send, recv, ssem, rsem = (xs, xr, xs_sem, xr_sem) if axis == "sx" else (ys, yr, ys_sem, yr_sem)
        other = jnp.maximum(pos[axis] - 1, 0) if side == 0 else jnp.minimum(pos[axis] + 1, (nsx if axis == "sx" else nsy) - 1)
        return pltpu.make_async_remote_copy(
            send.at[side, chunk(c)], recv.at[1 - side, chunk(c)], ssem.at[side, c], rsem.at[1 - side, c],
            device_id={axis: other}, device_id_type=MESH,
        )

    def halo_recv(axis, side, c):
        send, recv, ssem, rsem = (xs, xr, xs_sem, xr_sem) if axis == "sx" else (ys, yr, ys_sem, yr_sem)
        other = jnp.maximum(pos[axis] - 1, 0) if side == 0 else jnp.minimum(pos[axis] + 1, (nsx if axis == "sx" else nsy) - 1)
        return pltpu.make_async_remote_copy(
            send.at[side, chunk(c)], recv.at[side, chunk(c)], ssem.at[side, c], rsem.at[side, c],
            device_id={axis: other}, device_id_type=MESH,
        )

    def par_copy(c):
        return pltpu.make_async_remote_copy(
            snap.at[chunk(c)], peer.at[chunk(c)], ps_sem.at[c], pr_sem.at[c],
            device_id={"par": 1 - par}, device_id_type=MESH,
        )

    def fin_copy(c):
        return pltpu.make_async_copy(u_in.at[chunk(c)], fin_hbm.at[chunk(c)], fo_sem.at[c])

    @pl.loop(0, NC)
    def _(c):
        for cp in load(c):
            cp.start()

    psi_load = pltpu.make_async_copy(psi_hbm, psi, aux_sem.at[0])
    prev_load = pltpu.make_async_copy(prev_hbm, prev, aux_sem.at[1])
    psi_load.start()
    prev_load.start()

    barrier = pltpu.get_barrier_semaphore()
    for d in range(1, nsx):
        pl.semaphore_signal(barrier, inc=1, device_id={"sx": lax.rem(sx + d, nsx)}, device_id_type=MESH)
    for d in range(1, nsy):
        pl.semaphore_signal(barrier, inc=1, device_id={"sy": lax.rem(sy + d, nsy)}, device_id_type=MESH)
    pl.semaphore_signal(barrier, inc=1, device_id={"par": 1 - par}, device_id_type=MESH)

    for side in (0, 1):
        @pl.when(jnp.logical_not(has["sx", side]))
        def _():
            @pl.loop(0, S)
            def _(s):
                xr[side, s] = jnp.zeros(xr.shape[2:], BF16)

        @pl.when(jnp.logical_not(has["sy", side]))
        def _():
            @pl.loop(0, S)
            def _(s):
                yr[side, s] = jnp.zeros(yr.shape[2:], BF16)

    row8 = lax.broadcasted_iota(jnp.int32, (1, 8, Z), 1)
    low4 = row8 < 4
    yrow = lax.broadcasted_iota(jnp.int32, (1, Y + 2 * H, Z), 1)
    lane = lax.broadcasted_iota(jnp.int32, (1, Y + 2 * H, Z), 2)
    cut = ((yrow == H - 1) & (sy == 0)) | ((yrow == H + Y - 1) & (sy == nsy - 1))
    ymask = jnp.where(cut, 0.0, 1.0).astype(F32)

    pl.semaphore_wait(barrier, nsx + nsy - 1)

    @pl.loop(0, NC)
    def _(c):
        for cp in load(c):
            cp.wait()

        @pl.loop(0, CHUNK)
        def _(j):
            s = c * CHUNK + j
            for side, at in ((0, 0), (1, X - H)):
                xs[side, s, 0:H] = u_in[s, at:at + H].astype(BF16)
                xs[side, s, H:2 * H] = k_in[s, at:at + H].astype(BF16)

        for side in (0, 1):
            @pl.when(has["sx", side])
            def _():
                halo("sx", side, c).start()

    def half(s, x0, n, tile):
        rows = slice(8 * tile, 8 * tile + 8)
        if x0 < H:
            v = xr[0, s].astype(F32)
            return v[0:H, rows], v[H:2 * H, rows]
        if x0 >= H + X:
            v = xr[1, s].astype(F32)
            return v[0:H, rows], v[H:2 * H, rows]
        return u_in[s, x0 - H:x0 - H + n, rows], k_in[s, x0 - H:x0 - H + n, rows]

    groups = [(x0, H) for x0 in range(0, XE, H)]

    def y_edges(c):
        for side in (0, 1):
            @pl.when(has["sx", side])
            def _():
                halo_recv("sx", side, c).wait_recv()

        @pl.loop(0, CHUNK)
        def _(j):
            s = c * CHUNK + j
            for x0, n in groups:
                u0, k0 = half(s, x0, n, 0)
                u1, k1 = half(s, x0, n, 1)
                p = jnp.where(low4, k0, pltpu.roll(u0, 4, 1))
                q = jnp.where(low4, pltpu.roll(u1, 4, 1), k1)
                ys[0, s, x0 // 2:x0 // 2 + n // 2] = p.reshape(n // 2, 16, Z).astype(BF16)
                ys[1, s, x0 // 2:x0 // 2 + n // 2] = q.reshape(n // 2, 16, Z).astype(BF16)

        for side in (0, 1):
            @pl.when(has["sy", side])
            def _():
                halo("sy", side, c).start()

    def zshift(v, by):
        return pltpu.roll(v, by % Z, 2)

    def yshift(v, by):
        return pltpu.roll(v, by % v.shape[1], 1)

    def sample(s):
        for x0, n in groups:
            u0, k0 = half(s, x0, n, 0)
            u1, k1 = half(s, x0, n, 1)
            lo = yr[0, s, x0 // 2:x0 // 2 + n // 2].astype(F32).reshape(n, 8, Z)
            hi = yr[1, s, x0 // 2:x0 // 2 + n // 2].astype(F32).reshape(n, 8, Z)
            a, b = pltpu.roll(u0, 4, 1), pltpu.roll(u1, 4, 1)
            ua[x0:x0 + n, 0:8] = jnp.where(low4, lo, a)
            ua[x0:x0 + n, 8:16] = jnp.where(low4, a, b)
            ua[x0:x0 + n, 16:24] = jnp.where(low4, b, hi)
            a, b = pltpu.roll(k0, 4, 1), pltpu.roll(k1, 4, 1)
            kk[x0:x0 + n, 0:8] = jnp.where(low4, pltpu.roll(lo, 4, 1), a) * 0.08
            kk[x0:x0 + n, 8:16] = jnp.where(low4, a, b) * 0.08
            kk[x0:x0 + n, 16:24] = jnp.where(low4, b, pltpu.roll(hi, 4, 1)) * 0.08

        cx[0:1] = kk[0:1] + kk[1:2]

        def faces(i, _):
            x = pl.ds(1 + 2 * i, 2)
            k = kk[x]
            fx = k + kk[pl.ds(2 + 2 * i, 2)]
            bx = k + kk[pl.ds(2 * i, 2)]
            fy = k + yshift(k, -1)
            by = yshift(fy, 1)
            fz = k + jnp.where(lane < Z - 1, zshift(k, -1), 0.0)
            bz = k + jnp.where(lane > 0, zshift(k, 1), 0.0)
            dd[x] = 1.0 - (((fx + bx) + (fy + by)) + (fz + bz))
            cx[x] = fx
            cy[x] = fy * ymask
            cz[x] = jnp.where(lane < Z - 1, fz, 0.0)
            return 0

        lax.fori_loop(0, (XE - 2) // 2, faces, 0, unroll=True)

        @pl.when(sx == 0)
        def _():
            cx[H - 1:H] = jnp.zeros((1, Y + 2 * H, Z), F32)

        @pl.when(sx == nsx - 1)
        def _():
            cx[H + X - 1:H + X] = jnp.zeros((1, Y + 2 * H, Z), F32)

        def stencil(src, x0):
            x = pl.ds(x0, 2)
            u = src[x]
            y_c, z_c = cy[x], cz[x]
            out = dd[x] * u
            out += cx[x] * src[pl.ds(x0 + 1, 2)] + cx[pl.ds(x0 - 1, 2)] * src[pl.ds(x0 - 1, 2)]
            out += y_c * yshift(u, -1) + yshift(y_c * u, 1)
            out += z_c * zshift(u, -1) + zshift(z_c * u, 1)
            return out

        src, dst = ua, ub
        for step in range(STEPS - 1):
            first = 1 + step

            def advance(i, _, src=src, dst=dst, first=first):
                dst[pl.ds(first + 2 * i, 2)] = stencil(src, first + 2 * i)
                return 0

            lax.fori_loop(0, (XE - 2 * first) // 2, advance, 0, unroll=True)
            src, dst = dst, src

        def last(i, _, src=src):
            v = stencil(src, H + 2 * i)
            v0, v1, v2 = (pltpu.roll(v[:, 8 * t:8 * t + 8], 4, 1) for t in range(3))
            a, b = jnp.where(low4, v0, v1), jnp.where(low4, v1, v2)
            o = jnp.concatenate([a, b], axis=1)
            u_in[s, pl.ds(2 * i, 2)] = o
            snap[s, pl.ds(2 * i, 2)] = o.astype(BF16)
            return 0

        lax.fori_loop(0, X // 2, last, 0, unroll=True)

    y_edges(0)
    y_edges(1)

    i_r = lax.broadcasted_iota(jnp.int32, (RD * Y, R), 0) // Y
    i_j = lax.broadcasted_iota(jnp.int32, (RD * Y, R), 1)
    pick = jnp.where(i_j == i_r + par * RD, 1.0, 0.0).astype(BF16)
    cols = lax.dot_general(pick, omega_ref[...], (((1,), (1,)), ((), ())), preferred_element_type=F32).astype(BF16)
    total = omega_ref.shape[0]
    WB = 256

    @pl.loop(0, total * Y // WB)
    def _(b):
        e_s = lax.broadcasted_iota(jnp.int32, (total, WB), 0)
        e_c = lax.broadcasted_iota(jnp.int32, (total, WB), 1) + b * WB
        spread = jnp.where(e_s == lax.rem(e_c // Y + par * S, total), 1.0, 0.0).astype(BF16)
        wide = jnp.dot(cols, spread, preferred_element_type=F32)
        w_r = lax.rem(lax.broadcasted_iota(jnp.int32, (RD * Y, WB), 0), Y)
        w_c = lax.rem(lax.broadcasted_iota(jnp.int32, (RD * Y, WB), 1), Y)
        w_ref[:, pl.ds(pl.multiple_of(b * WB, WB), WB)] = jnp.where(w_r == w_c, wide, 0.0).astype(BF16)

    @pl.loop(0, NC)
    def _(c):
        @pl.when(c + 2 < NC)
        def _():
            y_edges(c + 2)

        for side in (0, 1):
            @pl.when(has["sy", side])
            def _():
                halo_recv("sy", side, c).wait_recv()

        @pl.loop(0, CHUNK)
        def _(j):
            sample(c * CHUNK + j)

        par_copy(c).start()
        fin_copy(c).start()

    psi_load.wait()
    SB, RB = 16, 16

    @pl.loop(0, (R // RB) * (S // SB))
    def _(b):
        rb, sb = b // (S // SB), lax.rem(b, S // SB)
        val = None
        for x in range(0, X, 2):
            left = jnp.concatenate([psi[pl.ds(rb * RB, RB), x + d].reshape(RB * Y, Z) for d in range(2)], axis=1)
            right = jnp.concatenate([snap[pl.ds(sb * SB, SB), x + d].reshape(SB * Y, Z) for d in range(2)], axis=1)
            term = lax.dot_general(left, right, (((1,), (1,)), ((), ())), preferred_element_type=F32)
            val = term if val is None else val + term
        w_r = lax.rem(lax.broadcasted_iota(jnp.int32, (RB * Y, SB * Y), 0), Y)
        w_c = lax.rem(lax.broadcasted_iota(jnp.int32, (RB * Y, SB * Y), 1), Y)
        val = jnp.where(w_r == w_c, val, 0.0).reshape(RB, Y, SB * Y)
        red[sb, pl.ds(rb * RB, RB)] = jnp.sum(val, axis=1)

    Q = Z // S
    RQ = R // Q
    dense = jnp.zeros((RQ, Z), F32)
    for q in range(Q):
        for sb in range(S // SB):
            g_c = lax.broadcasted_iota(jnp.int32, (SB * Y, Z), 0) // Y + sb * SB + q * S
            g_l = lax.broadcasted_iota(jnp.int32, (SB * Y, Z), 1)
            group = jnp.where(g_c == g_l, 1.0, 0.0).astype(F32)
            dense += jnp.dot(red[sb, q * RQ:(q + 1) * RQ], group, preferred_element_type=F32, precision=lax.Precision.HIGHEST)
    part[...] = dense

    def gather(axis, d, src, dst, ssem, rsem):
        n = dst.shape[0]
        to = lax.rem(pos[axis] + d, n)
        frm = lax.rem(pos[axis] + n - d, n)
        out = pltpu.make_async_remote_copy(
            src, dst.at[pos[axis]], ssem.at[d], rsem.at[d], device_id={axis: to}, device_id_type=MESH)
        inn = pltpu.make_async_remote_copy(
            src, dst.at[frm], ssem.at[d], rsem.at[d], device_id={axis: to}, device_id_type=MESH)
        return out, inn

    for d in range(1, nsx):
        gather("sx", d, part, gat1, a1s_sem, a1r_sem)[0].start()

    prev_load.wait()

    def range_part(x0, weights, source, lo, n):
        right = jnp.concatenate([source[lo:lo + n, x0 + d].reshape(n * Y, Z) for d in range(2)], axis=1)
        return jnp.dot(weights, right, preferred_element_type=F32)

    for x0 in range(0, X, 2):
        t = range_part(x0, w_ref[:, 0:S * Y], snap, 0, S)
        for d in range(2):
            acc[x0 + d] = prev[:, x0 + d].reshape(RD * Y, Z).astype(F32) + t[:, d * Z:(d + 1) * Z]

    gat1[pl.ds(sx, 1)] = part[...][None]
    for d in range(1, nsx):
        out, inn = gather("sx", d, part, gat1, a1s_sem, a1r_sem)
        out.wait_send()
        inn.wait_recv()
    tot = gat1[0]
    for i in range(1, nsx):
        tot += gat1[i]
    part2[...] = tot
    for d in range(1, nsy):
        gather("sy", d, part2, gat2, a2s_sem, a2r_sem)[0].start()

    HALF = S // 2
    for c in range(NC // 2):
        par_copy(c).wait_recv()
    for x0 in range(0, X, 2):
        t = range_part(x0, w_ref[:, S * Y:(S + HALF) * Y], peer, 0, HALF)
        for d in range(2):
            acc[x0 + d] = acc[x0 + d] + t[:, d * Z:(d + 1) * Z]

    gat2[pl.ds(sy, 1)] = part2[...][None]
    for d in range(1, nsy):
        out, inn = gather("sy", d, part2, gat2, a2s_sem, a2r_sem)
        out.wait_send()
        inn.wait_recv()
    tot = gat2[0]
    for i in range(1, nsy):
        tot += gat2[i]
    for q in range(Q):
        cor_ref[q * RQ:(q + 1) * RQ] = cprev_ref[q * RQ:(q + 1) * RQ] + tot[:, q * S:(q + 1) * S]

    for c in range(NC // 2, NC):
        par_copy(c).wait_recv()

    def range_out(x0):
        return pltpu.make_async_copy(rout.at[:, pl.ds(x0, 2)], range_hbm.at[:, pl.ds(x0, 2)], ro_sem.at[x0 // 2])

    for x0 in range(0, X, 2):
        t = range_part(x0, w_ref[:, (S + HALF) * Y:2 * S * Y], peer, HALF, HALF)
        for d in range(2):
            v = acc[x0 + d] + t[:, d * Z:(d + 1) * Z]
            rout[:, x0 + d] = v.astype(BF16).reshape(RD, Y, Z)
        range_out(x0).start()

    @pl.loop(0, NC)
    def _(c):
        for side in (0, 1):
            for axis in ("sx", "sy"):
                @pl.when(has[axis, side])
                def _():
                    halo(axis, side, c).wait_send()
        par_copy(c).wait_send()
        fin_copy(c).wait()

    for x0 in range(0, X, 2):
        range_out(x0).wait()


def per_device(sizes, initial_state, conductivity, omega, psi, range_prev, corange_prev):
    S, X, Y, Z = initial_state.shape
    R, RD = psi.shape[0], range_prev.shape[0]
    nsx, nsy = sizes
    NC = S // CHUNK
    E = (X + 2 * H, Y + 2 * H, Z)
    dma = pltpu.SemaphoreType.DMA
    scratch = [
        pltpu.VMEM((S, X, Y, Z), F32),
        pltpu.VMEM((S, X, Y, Z), F32),
        pltpu.VMEM((2, S, 2 * H, Y, Z), BF16),
        pltpu.VMEM((2, S, 2 * H, Y, Z), BF16),
        pltpu.VMEM((2, S, E[0] // 2, 16, Z), BF16),
        pltpu.VMEM((2, S, E[0] // 2, 16, Z), BF16),
        pltpu.VMEM((S, X, Y, Z), BF16),
        pltpu.VMEM((S, X, Y, Z), BF16),
        pltpu.VMEM((R, X, Y, Z), BF16),
        pltpu.VMEM((RD, X, Y, Z), BF16),
        pltpu.VMEM((X, RD * Y, Z), F32),
        pltpu.VMEM((RD * Y, 2 * S * Y), BF16),
        pltpu.VMEM((S // 16, R, 16 * Y), F32),
        pltpu.VMEM((R * S // Z, Z), F32),
        pltpu.VMEM((nsx, R * S // Z, Z), F32),
        pltpu.VMEM((R * S // Z, Z), F32),
        pltpu.VMEM((nsy, R * S // Z, Z), F32),
    ] + [pltpu.VMEM(E, F32)] * 7 + [
        pltpu.VMEM((RD, X, Y, Z), BF16),
        dma((2, NC)), dma((2,)), dma((2, NC)), dma((2, NC)), dma((2, NC)), dma((2, NC)),
        dma((NC,)), dma((NC,)), dma((NC,)), dma((X // 2,)),
        dma((nsx,)), dma((nsx,)), dma((nsy,)), dma((nsy,)),
    ]
    any_ = pl.BlockSpec(memory_space=pl.ANY)
    vmem = pl.BlockSpec(memory_space=pltpu.VMEM)
    return pl.pallas_call(
        kernel,
        out_shape=(
            jax.ShapeDtypeStruct(initial_state.shape, F32),
            jax.ShapeDtypeStruct(range_prev.shape, BF16),
            jax.ShapeDtypeStruct(corange_prev.shape, F32),
        ),
        in_specs=[any_, any_, vmem, any_, any_, vmem],
        out_specs=(any_, any_, vmem),
        scratch_shapes=scratch,
        compiler_params=pltpu.CompilerParams(
            collective_id=0, has_side_effects=True, vmem_limit_bytes=60 * 2**20
        ),
    )(initial_state, conductivity, omega, psi, range_prev, corange_prev)


def solution(mesh):
    in_specs = (
        P("par", "sx", "sy", None),
        P("par", "sx", "sy", None),
        P(),
        P(None, "sx", "sy", None),
        P("par", "sx", "sy", None),
        P(None, "par"),
    )
    out_specs = (P("par", "sx", "sy", None), P("par", "sx", "sy", None), P(None, "par"))
    sizes = (mesh.shape["sx"], mesh.shape["sy"])
    return jax.shard_map(
        functools.partial(per_device, sizes), mesh=mesh, in_specs=in_specs, out_specs=out_specs, check_vma=False
    )
```

```python
import functools

import jax
import jax.numpy as jnp
from jax import lax
from jax.experimental import pallas as pl
from jax.experimental.pallas import tpu as pltpu
from jax.sharding import PartitionSpec as P

STEPS = 4
H = STEPS
MESH = pl.DeviceIdType.MESH
F32 = jnp.float32
BF16 = jnp.bfloat16
CHUNK = 2
AHEAD = 16
HELD = 4
VMEM_MIB = 44


def kernel(
    u_hbm, k_hbm, omega_ref, psi_hbm, prev_hbm, cprev_ref,
    u_in, rout, cor_ref,
    k_in, xs, xr, rly, ys, yr, snap, peer, psi, prev, acc, w_ref, red, part, gat1, part2, gat2,
    ua, ub, kk, cx, cy, cz, dd,
    load_sem, aux_sem, xs_sem, xr_sem, ry_sem, rf_sem, ys_sem, yr_sem, ps_sem, pr_sem,
    a1s_sem, a1r_sem, a2s_sem, a2r_sem,
):
    S, X, Y, Z = u_in.shape
    NC = S // CHUNK
    XE = X + 2 * H
    R = psi.shape[0]
    RD = prev.shape[0]
    sx, sy, par = lax.axis_index("sx"), lax.axis_index("sy"), lax.axis_index("par")
    nsx, nsy = gat1.shape[0], gat2.shape[0]
    has = {("sx", 0): sx > 0, ("sx", 1): sx < nsx - 1, ("sy", 0): sy > 0, ("sy", 1): sy < nsy - 1}
    pos = {"sx": sx, "sy": sy}

    def chunk(c):
        return pl.ds(c * CHUNK, CHUNK)

    def load(c):
        return (
            pltpu.make_async_copy(u_hbm.at[chunk(c)], u_in.at[chunk(c)], load_sem.at[0, c]),
            pltpu.make_async_copy(k_hbm.at[chunk(c)], k_in.at[chunk(c)], load_sem.at[1, c]),
        )

    XW = nsx // 2

    def remote(src, dst, ssem, rsem, axis, other):
        return pltpu.make_async_remote_copy(src, dst, ssem, rsem, device_id={axis: other}, device_id_type=MESH)

    def beside(axis, side):
        n = nsx if axis == "sx" else nsy
        return jnp.maximum(pos[axis] - 1, 0) if side == 0 else jnp.minimum(pos[axis] + 1, n - 1)

    def halo(axis, side, c):
        send, recv, ssem, rsem = (xs, xr, xs_sem, xr_sem) if axis == "sx" else (ys, yr, ys_sem, yr_sem)
        return remote(send.at[side, chunk(c)], recv.at[1 - side, chunk(c)], ssem.at[side, c], rsem.at[1 - side, c],
                      axis, beside(axis, side))

    def halo_recv(axis, side, c):
        send, recv, ssem, rsem = (xs, xr, xs_sem, xr_sem) if axis == "sx" else (ys, yr, ys_sem, yr_sem)
        return remote(send.at[side, chunk(c)], recv.at[side, chunk(c)], ssem.at[side, c], rsem.at[side, c],
                      axis, beside(axis, side))

    def detour(side, c):
        q = lax.rem(c, 2) * (XW - 1)
        at_seam = (sx == XW - 1) if side == 1 else (sx == XW)
        via = XW + q if side == 1 else XW - 1 - q
        return at_seam & (q != 0), via, c // 2

    def to_relay(side, c):
        _, via, m = detour(side, c)
        return remote(xs.at[side, chunk(c)], rly.at[m], xs_sem.at[side, c], ry_sem.at[m], "sx", via)

    def relay(c):
        q = lax.rem(c, 2) * (XW - 1)
        m = c // 2
        for side in (0, 1):
            mine = ((sx == XW + q) if side == 1 else (sx == XW - 1 - q)) & (q != 0)

            @pl.when(mine & (c < NC))
            def _():
                dest = XW if side == 1 else XW - 1
                cp = remote(rly.at[m], xr.at[1 - side, chunk(c)], rf_sem.at[m], xr_sem.at[1 - side, c], "sx", dest)
                remote(rly.at[m], rly.at[m], rf_sem.at[m], ry_sem.at[m], "sx", dest).wait_recv()
                cp.start()

    def relay_done(c):
        q = lax.rem(c, 2) * (XW - 1)
        m = c // 2
        for side in (0, 1):
            mine = ((sx == XW + q) if side == 1 else (sx == XW - 1 - q)) & (q != 0)

            @pl.when(mine)
            def _():
                dest = XW if side == 1 else XW - 1
                remote(rly.at[m], xr.at[1 - side, chunk(c)], rf_sem.at[m], xr_sem.at[1 - side, c], "sx", dest).wait_send()

    def par_copy(c):
        return pltpu.make_async_remote_copy(
            snap.at[chunk(c)], peer.at[chunk(c)], ps_sem.at[c], pr_sem.at[c],
            device_id={"par": 1 - par}, device_id_type=MESH,
        )

    @pl.loop(0, NC)
    def _(c):
        for cp in load(c):
            cp.start()

    psi_load = pltpu.make_async_copy(psi_hbm, psi, aux_sem.at[0])
    prev_load = pltpu.make_async_copy(prev_hbm, prev, aux_sem.at[1])
    psi_load.start()
    prev_load.start()

    barrier = pltpu.get_barrier_semaphore()
    for d in range(1, nsx):
        pl.semaphore_signal(barrier, inc=1, device_id={"sx": lax.rem(sx + d, nsx)}, device_id_type=MESH)
    for d in range(1, nsy):
        pl.semaphore_signal(barrier, inc=1, device_id={"sy": lax.rem(sy + d, nsy)}, device_id_type=MESH)
    pl.semaphore_signal(barrier, inc=1, device_id={"par": 1 - par}, device_id_type=MESH)

    for side in (0, 1):
        @pl.when(jnp.logical_not(has["sx", side]))
        def _():
            @pl.loop(0, S)
            def _(s):
                xr[side, s] = jnp.zeros(xr.shape[2:], BF16)

        @pl.when(jnp.logical_not(has["sy", side]))
        def _():
            @pl.loop(0, S)
            def _(s):
                yr[side, s] = jnp.zeros(yr.shape[2:], BF16)

    row8 = lax.broadcasted_iota(jnp.int32, (1, 8, Z), 1)
    low4 = row8 < 4
    yrow = lax.broadcasted_iota(jnp.int32, (1, Y + 2 * H, Z), 1)
    lane = lax.broadcasted_iota(jnp.int32, (1, Y + 2 * H, Z), 2)
    cut = ((yrow == H - 1) & (sy == 0)) | ((yrow == H + Y - 1) & (sy == nsy - 1))
    ymask = jnp.where(cut, 0.0, 1.0).astype(F32)

    pl.semaphore_wait(barrier, nsx + nsy - 1)

    def x_edges(c):
        for cp in load(c):
            cp.wait()

        @pl.loop(0, CHUNK)
        def _(j):
            s = c * CHUNK + j
            for side, at in ((0, 0), (1, X - H)):
                xs[side, s, 0:H] = u_in[s, at:at + H].astype(BF16)
                xs[side, s, H:2 * H] = k_in[s, at:at + H].astype(BF16)

        for side in (0, 1):
            turn = detour(side, c)[0]

            @pl.when(has["sx", side] & turn)
            def _():
                to_relay(side, c).start()

            @pl.when(has["sx", side] & jnp.logical_not(turn))
            def _():
                halo("sx", side, c).start()

    @pl.loop(0, AHEAD)
    def _(c):
        x_edges(c)

    def half(s, x0, n, tile):
        rows = slice(8 * tile, 8 * tile + 8)
        if x0 < H:
            v = xr[0, s].astype(F32)
            return v[0:H, rows], v[H:2 * H, rows]
        if x0 >= H + X:
            v = xr[1, s].astype(F32)
            return v[0:H, rows], v[H:2 * H, rows]
        return u_in[s, x0 - H:x0 - H + n, rows], k_in[s, x0 - H:x0 - H + n, rows]

    groups = [(x0, H) for x0 in range(0, XE, H)]

    def y_edges(c):
        for side in (0, 1):
            @pl.when(has["sx", side])
            def _():
                halo_recv("sx", side, c).wait_recv()

        @pl.loop(0, CHUNK)
        def _(j):
            s = c * CHUNK + j
            for x0, n in groups:
                u0, k0 = half(s, x0, n, 0)
                u1, k1 = half(s, x0, n, 1)
                p = jnp.where(low4, k0, pltpu.roll(u0, 4, 1))
                q = jnp.where(low4, pltpu.roll(u1, 4, 1), k1)
                ys[0, s, x0 // 2:x0 // 2 + n // 2] = p.reshape(n // 2, 16, Z).astype(BF16)
                ys[1, s, x0 // 2:x0 // 2 + n // 2] = q.reshape(n // 2, 16, Z).astype(BF16)

        for side in (0, 1):
            @pl.when(has["sy", side])
            def _():
                halo("sy", side, c).start()

    def zshift(v, by):
        return pltpu.roll(v, by % Z, 2)

    def yshift(v, by):
        return pltpu.roll(v, by % v.shape[1], 1)

    def sample(s):
        for x0, n in groups:
            u0, k0 = half(s, x0, n, 0)
            u1, k1 = half(s, x0, n, 1)
            lo = yr[0, s, x0 // 2:x0 // 2 + n // 2].astype(F32).reshape(n, 8, Z)
            hi = yr[1, s, x0 // 2:x0 // 2 + n // 2].astype(F32).reshape(n, 8, Z)
            a, b = pltpu.roll(u0, 4, 1), pltpu.roll(u1, 4, 1)
            ua[x0:x0 + n, 0:8] = jnp.where(low4, lo, a)
            ua[x0:x0 + n, 8:16] = jnp.where(low4, a, b)
            ua[x0:x0 + n, 16:24] = jnp.where(low4, b, hi)
            a, b = pltpu.roll(k0, 4, 1), pltpu.roll(k1, 4, 1)
            kk[x0:x0 + n, 0:8] = jnp.where(low4, pltpu.roll(lo, 4, 1), a) * 0.08
            kk[x0:x0 + n, 8:16] = jnp.where(low4, a, b) * 0.08
            kk[x0:x0 + n, 16:24] = jnp.where(low4, b, pltpu.roll(hi, 4, 1)) * 0.08

        cx[0:1] = kk[0:1] + kk[1:2]

        def faces(i, _):
            x = pl.ds(1 + 2 * i, 2)
            k = kk[x]
            fx = k + kk[pl.ds(2 + 2 * i, 2)]
            bx = k + kk[pl.ds(2 * i, 2)]
            fy = k + yshift(k, -1)
            by = yshift(fy, 1)
            fz = k + jnp.where(lane < Z - 1, zshift(k, -1), 0.0)
            bz = k + jnp.where(lane > 0, zshift(k, 1), 0.0)
            dd[x] = 1.0 - (((fx + bx) + (fy + by)) + (fz + bz))
            cx[x] = fx
            cy[x] = fy * ymask
            cz[x] = jnp.where(lane < Z - 1, fz, 0.0)
            return 0

        lax.fori_loop(0, (XE - 2) // 2, faces, 0, unroll=True)

        @pl.when(sx == 0)
        def _():
            cx[H - 1:H] = jnp.zeros((1, Y + 2 * H, Z), F32)

        @pl.when(sx == nsx - 1)
        def _():
            cx[H + X - 1:H + X] = jnp.zeros((1, Y + 2 * H, Z), F32)

        def stencil(src, x0):
            x = pl.ds(x0, 2)
            u = src[x]
            y_c, z_c = cy[x], cz[x]
            out = dd[x] * u
            out += cx[x] * src[pl.ds(x0 + 1, 2)] + cx[pl.ds(x0 - 1, 2)] * src[pl.ds(x0 - 1, 2)]
            out += y_c * yshift(u, -1) + yshift(y_c * u, 1)
            out += z_c * zshift(u, -1) + zshift(z_c * u, 1)
            return out

        src, dst = ua, ub
        for step in range(STEPS - 1):
            first = 1 + step

            def advance(i, _, src=src, dst=dst, first=first):
                dst[pl.ds(first + 2 * i, 2)] = stencil(src, first + 2 * i)
                return 0

            lax.fori_loop(0, (XE - 2 * first) // 2, advance, 0, unroll=True)
            src, dst = dst, src

        def last(i, _, src=src):
            v = stencil(src, H + 2 * i)
            v0, v1, v2 = (pltpu.roll(v[:, 8 * t:8 * t + 8], 4, 1) for t in range(3))
            a, b = jnp.where(low4, v0, v1), jnp.where(low4, v1, v2)
            o = jnp.concatenate([a, b], axis=1)
            u_in[s, pl.ds(2 * i, 2)] = o
            snap[s, pl.ds(2 * i, 2)] = o.astype(BF16)
            return 0

        lax.fori_loop(0, X // 2, last, 0, unroll=True)

    y_edges(0)
    relay(jnp.int32(1))
    relay(jnp.int32(2))
    y_edges(1)

    i_r = lax.broadcasted_iota(jnp.int32, (RD * Y, R), 0) // Y
    i_j = lax.broadcasted_iota(jnp.int32, (RD * Y, R), 1)
    pick = jnp.where(i_j == i_r + par * RD, 1.0, 0.0).astype(BF16)
    cols = lax.dot_general(pick, omega_ref[...], (((1,), (1,)), ((), ())), preferred_element_type=F32).astype(BF16)
    total = omega_ref.shape[0]
    WB = 256

    @pl.loop(0, total * Y // WB)
    def _(b):
        e_s = lax.broadcasted_iota(jnp.int32, (total, WB), 0)
        e_c = lax.broadcasted_iota(jnp.int32, (total, WB), 1) + b * WB
        spread = jnp.where(e_s == lax.rem(e_c // Y + par * S, total), 1.0, 0.0).astype(BF16)
        wide = jnp.dot(cols, spread, preferred_element_type=F32)
        w_r = lax.rem(lax.broadcasted_iota(jnp.int32, (RD * Y, WB), 0), Y)
        w_c = lax.rem(lax.broadcasted_iota(jnp.int32, (RD * Y, WB), 1), Y)
        w_ref[:, pl.ds(pl.multiple_of(b * WB, WB), WB)] = jnp.where(w_r == w_c, wide, 0.0).astype(BF16)

    SB, RB = 16, 16

    def corange(sb):
        @pl.loop(0, R // RB)
        def _(rb):
            val = None
            for x in range(0, X, 2):
                left = jnp.concatenate([psi[pl.ds(rb * RB, RB), x + d].reshape(RB * Y, Z) for d in range(2)], axis=1)
                right = jnp.concatenate([snap[pl.ds(sb * SB, SB), x + d].reshape(SB * Y, Z) for d in range(2)], axis=1)
                term = lax.dot_general(left, right, (((1,), (1,)), ((), ())), preferred_element_type=F32)
                val = term if val is None else val + term
            w_r = lax.rem(lax.broadcasted_iota(jnp.int32, (RB * Y, SB * Y), 0), Y)
            w_c = lax.rem(lax.broadcasted_iota(jnp.int32, (RB * Y, SB * Y), 1), Y)
            val = jnp.where(w_r == w_c, val, 0.0).reshape(RB, Y, SB * Y)
            red[sb, pl.ds(rb * RB, RB)] = jnp.sum(val, axis=1)

    psi_load.wait()

    @pl.loop(0, NC)
    def _(c):
        for sb in range(S // SB - 1):
            @pl.when(c == (sb + 1) * SB // CHUNK)
            def _():
                corange(sb)

        @pl.when(c + AHEAD < NC)
        def _():
            x_edges(c + AHEAD)

        upto = jnp.minimum(2 * c + 4, c + 8)

        @pl.loop(jnp.minimum(2 * c + 2, c + 8 - 1) + 1, upto + 1)
        def _(i):
            relay(i)

        @pl.when(c + 2 < NC)
        def _():
            y_edges(c + 2)

        for side in (0, 1):
            @pl.when(has["sy", side])
            def _():
                halo_recv("sy", side, c).wait_recv()

        @pl.loop(0, CHUNK)
        def _(j):
            sample(c * CHUNK + j)

        @pl.when(c < NC - HELD)
        def _():
            par_copy(c).start()

    corange(S // SB - 1)

    g_r = lax.broadcasted_iota(jnp.int32, (SB, SB * Y), 0)
    g_c = lax.broadcasted_iota(jnp.int32, (SB, SB * Y), 1) // Y
    group = jnp.where(g_r == g_c, 1.0, 0.0).astype(F32)
    part[...] = jnp.concatenate([
        lax.dot_general(group, red[q], (((1,), (1,)), ((), ())), preferred_element_type=F32, precision=lax.Precision.HIGHEST)
        for q in range(S // SB)], axis=1)

    def gather(axis, d, src, dst, ssem, rsem):
        n = dst.shape[0]
        return remote(src, dst.at[pos[axis]], ssem.at[d], rsem.at[d], axis, lax.rem(pos[axis] + d, n))

    def gather_recv(axis, d, src, dst, ssem, rsem):
        n = dst.shape[0]
        return remote(src, dst.at[lax.rem(pos[axis] + n - d, n)], ssem.at[d], rsem.at[d], axis, lax.rem(pos[axis] + d, n))

    for d in range(1, nsx):
        gather("sx", d, part, gat1, a1s_sem, a1r_sem).start()

    @pl.loop(NC - HELD, NC)
    def _(c):
        par_copy(c).start()

    prev_load.wait()

    def range_part(x0, weights, source, lo, n):
        right = jnp.concatenate([source[lo:lo + n, x0 + d].reshape(n * Y, Z) for d in range(2)], axis=1)
        return jnp.dot(weights, right, preferred_element_type=F32)

    for x0 in range(0, X, 2):
        t = range_part(x0, w_ref[:, 0:S * Y], snap, 0, S)
        for d in range(2):
            acc[x0 + d] = prev[:, x0 + d].reshape(RD * Y, Z).astype(F32) + t[:, d * Z:(d + 1) * Z]

    gat1[pl.ds(sx, 1)] = part[...][None]
    for d in range(1, nsx):
        gather("sx", d, part, gat1, a1s_sem, a1r_sem).wait_send()
        gather_recv("sx", d, part, gat1, a1s_sem, a1r_sem).wait_recv()
    tot = gat1[0]
    for i in range(1, nsx):
        tot += gat1[i]
    part2[...] = tot
    for d in range(1, nsy):
        gather("sy", d, part2, gat2, a2s_sem, a2r_sem).start()

    HALF = S // 2
    for c in range(NC // 2):
        par_copy(c).wait_recv()
    for x0 in range(0, X, 2):
        t = range_part(x0, w_ref[:, S * Y:(S + HALF) * Y], peer, 0, HALF)
        for d in range(2):
            acc[x0 + d] = acc[x0 + d] + t[:, d * Z:(d + 1) * Z]

    gat2[pl.ds(sy, 1)] = part2[...][None]
    for d in range(1, nsy):
        gather("sy", d, part2, gat2, a2s_sem, a2r_sem).wait_send()
        gather_recv("sy", d, part2, gat2, a2s_sem, a2r_sem).wait_recv()
    tot = gat2[0]
    for i in range(1, nsy):
        tot += gat2[i]
    for q in range(S // SB):
        cor_ref[q * SB:(q + 1) * SB] = cprev_ref[q * SB:(q + 1) * SB] + tot[:, q * R:(q + 1) * R]

    for c in range(NC // 2, NC):
        par_copy(c).wait_recv()

    for x0 in range(0, X, 2):
        t = range_part(x0, w_ref[:, (S + HALF) * Y:2 * S * Y], peer, HALF, HALF)
        for d in range(2):
            v = acc[x0 + d] + t[:, d * Z:(d + 1) * Z]
            rout[:, x0 + d] = v.astype(BF16).reshape(RD, Y, Z)

    @pl.loop(0, NC)
    def _(c):
        for side in (0, 1):
            for axis in ("sx", "sy"):
                @pl.when(has[axis, side])
                def _():
                    halo(axis, side, c).wait_send()
        relay_done(c)
        par_copy(c).wait_send()


def store(fin_ref, rng_ref, fin_hbm, rng_hbm, sem):
    parts = 4
    copies = []
    for i, (src, dst) in enumerate(((fin_ref, fin_hbm), (rng_ref, rng_hbm))):
        n = src.shape[0] // parts
        copies += [pltpu.make_async_copy(src.at[pl.ds(p * n, n)], dst.at[pl.ds(p * n, n)], sem.at[i, p]) for p in range(parts)]
    for cp in copies:
        cp.start()
    for cp in copies:
        cp.wait()


def per_device(sizes, initial_state, conductivity, omega, psi, range_prev, corange_prev):
    S, X, Y, Z = initial_state.shape
    R, RD = psi.shape[0], range_prev.shape[0]
    nsx, nsy = sizes
    NC = S // CHUNK
    E = (X + 2 * H, Y + 2 * H, Z)
    dma = pltpu.SemaphoreType.DMA
    scratch = [
        pltpu.VMEM((S, X, Y, Z), F32),
        pltpu.VMEM((2, S, 2 * H, Y, Z), BF16),
        pltpu.VMEM((2, S, 2 * H, Y, Z), BF16),
        pltpu.VMEM((NC // 2, CHUNK, 2 * H, Y, Z), BF16),
        pltpu.VMEM((2, S, E[0] // 2, 16, Z), BF16),
        pltpu.VMEM((2, S, E[0] // 2, 16, Z), BF16),
        pltpu.VMEM((S, X, Y, Z), BF16),
        pltpu.VMEM((S, X, Y, Z), BF16),
        pltpu.VMEM((R, X, Y, Z), BF16),
        pltpu.VMEM((RD, X, Y, Z), BF16),
        pltpu.VMEM((X, RD * Y, Z), F32),
        pltpu.VMEM((RD * Y, 2 * S * Y), BF16),
        pltpu.VMEM((S // 16, R, 16 * Y), F32),
        pltpu.VMEM((R * S // Z, Z), F32),
        pltpu.VMEM((nsx, R * S // Z, Z), F32),
        pltpu.VMEM((R * S // Z, Z), F32),
        pltpu.VMEM((nsy, R * S // Z, Z), F32),
    ] + [pltpu.VMEM(E, F32)] * 7 + [
        dma((2, NC)), dma((2,)), dma((2, NC)), dma((2, NC)), dma((NC // 2,)), dma((NC // 2,)),
        dma((2, NC)), dma((2, NC)), dma((NC,)), dma((NC,)),
        dma((nsx,)), dma((nsx,)), dma((nsy,)), dma((nsy,)),
    ]
    any_ = pl.BlockSpec(memory_space=pl.ANY)
    hbm = pl.BlockSpec(memory_space=pltpu.HBM)
    vmem = pl.BlockSpec(memory_space=pltpu.VMEM)
    final, sketch, corange = pl.pallas_call(
        kernel,
        out_shape=(
            jax.ShapeDtypeStruct(initial_state.shape, F32),
            jax.ShapeDtypeStruct(range_prev.shape, BF16),
            jax.ShapeDtypeStruct(corange_prev.shape[::-1], F32),
        ),
        in_specs=[hbm, hbm, vmem, hbm, hbm, vmem],
        out_specs=(vmem, vmem, vmem),
        scratch_shapes=scratch,
        compiler_params=pltpu.CompilerParams(
            collective_id=0, has_side_effects=True, vmem_limit_bytes=VMEM_MIB * 2**20
        ),
    )(initial_state, conductivity, omega, psi, range_prev, corange_prev.T)
    final, sketch = pl.pallas_call(
        store,
        out_shape=(
            jax.ShapeDtypeStruct(initial_state.shape, F32),
            jax.ShapeDtypeStruct(range_prev.shape, BF16),
        ),
        in_specs=[vmem, vmem],
        out_specs=(any_, any_),
        scratch_shapes=[dma((2, 4))],
        compiler_params=pltpu.CompilerParams(vmem_limit_bytes=8 * 2**20),
    )(final, sketch)
    return final, sketch, corange.T


def solution(mesh):
    in_specs = (
        P("par", "sx", "sy", None),
        P("par", "sx", "sy", None),
        P(),
        P(None, "sx", "sy", None),
        P("par", "sx", "sy", None),
        P(None, "par"),
    )
    out_specs = (P("par", "sx", "sy", None), P("par", "sx", "sy", None), P(None, "par"))
    sizes = (mesh.shape["sx"], mesh.shape["sy"])
    return jax.shard_map(
        functools.partial(per_device, sizes), mesh=mesh, in_specs=in_specs, out_specs=out_specs, check_vma=False
    )
```

```python
import functools

import jax
import jax.numpy as jnp
from jax import lax
from jax.experimental import pallas as pl
from jax.experimental.pallas import tpu as pltpu
from jax.sharding import PartitionSpec as P

STEPS = 4
H = STEPS
MESH = pl.DeviceIdType.MESH
F32 = jnp.float32
BF16 = jnp.bfloat16
CHUNK = 2
AHEAD = 16
HELD = 4
VMEM_MIB = 44
PIECES = 4
DETOUR = 1
LAG = 3


def kernel(
    u_hbm, k_hbm, omega_hbm, psi_hbm,
    u_in, acc, cor_ref,
    k_in, xs, xr, rly, rlp, ys, yr, snap, peer, psi, omega_ref, w_ref, red, part, gat1, part2, gat2,
    ua, ub, kk, cx, cy, cz, dd,
    load_sem, aux_sem, xs_sem, xr_sem, ry_sem, rf_sem, ys_sem, yr_sem, ps_sem, pr_sem, ds_sem, dr_sem,
    a1s_sem, a1r_sem, a2s_sem, a2r_sem,
):
    S, X, Y, Z = u_in.shape
    NC = S // CHUNK
    XE = X + 2 * H
    R = psi.shape[0]
    RD = acc.shape[1] // Y
    sx, sy, par = lax.axis_index("sx"), lax.axis_index("sy"), lax.axis_index("par")
    nsx, nsy = gat1.shape[0], gat2.shape[0]
    has = {("sx", 0): sx > 0, ("sx", 1): sx < nsx - 1, ("sy", 0): sy > 0, ("sy", 1): sy < nsy - 1}
    pos = {"sx": sx, "sy": sy}

    def chunk(c):
        return pl.ds(c * CHUNK, CHUNK)

    def load(c):
        return (
            pltpu.make_async_copy(u_hbm.at[chunk(c)], u_in.at[chunk(c)], load_sem.at[0, c]),
            pltpu.make_async_copy(k_hbm.at[chunk(c)], k_in.at[chunk(c)], load_sem.at[1, c]),
        )

    XW = nsx // 2

    def remote(src, dst, ssem, rsem, axis, other):
        return pltpu.make_async_remote_copy(src, dst, ssem, rsem, device_id={axis: other}, device_id_type=MESH)

    def beside(axis, side):
        n = nsx if axis == "sx" else nsy
        return jnp.maximum(pos[axis] - 1, 0) if side == 0 else jnp.minimum(pos[axis] + 1, n - 1)

    def halo(axis, side, c):
        send, recv, ssem, rsem = (xs, xr, xs_sem, xr_sem) if axis == "sx" else (ys, yr, ys_sem, yr_sem)
        return remote(send.at[side, chunk(c)], recv.at[1 - side, chunk(c)], ssem.at[side, c], rsem.at[1 - side, c],
                      axis, beside(axis, side))

    def halo_recv(axis, side, c):
        send, recv, ssem, rsem = (xs, xr, xs_sem, xr_sem) if axis == "sx" else (ys, yr, ys_sem, yr_sem)
        return remote(send.at[side, chunk(c)], recv.at[side, chunk(c)], ssem.at[side, c], rsem.at[side, c],
                      axis, beside(axis, side))

    def detour(side, c):
        q = lax.rem(c, 2) * (XW - 1)
        at_seam = (sx == XW - 1) if side == 1 else (sx == XW)
        via = XW + q if side == 1 else XW - 1 - q
        return at_seam & (q != 0), via, c // 2

    def to_relay(side, c):
        _, via, m = detour(side, c)
        return remote(xs.at[side, chunk(c)], rly.at[m], xs_sem.at[side, c], ry_sem.at[m], "sx", via)

    def relay(c):
        q = lax.rem(c, 2) * (XW - 1)
        m = c // 2
        for side in (0, 1):
            mine = ((sx == XW + q) if side == 1 else (sx == XW - 1 - q)) & (q != 0)

            @pl.when(mine & (c < NC))
            def _():
                dest = XW if side == 1 else XW - 1
                cp = remote(rly.at[m], xr.at[1 - side, chunk(c)], rf_sem.at[m], xr_sem.at[1 - side, c], "sx", dest)
                remote(rly.at[m], rly.at[m], rf_sem.at[m], ry_sem.at[m], "sx", dest).wait_recv()
                cp.start()

    def relay_done(c):
        q = lax.rem(c, 2) * (XW - 1)
        m = c // 2
        for side in (0, 1):
            mine = ((sx == XW + q) if side == 1 else (sx == XW - 1 - q)) & (q != 0)

            @pl.when(mine)
            def _():
                dest = XW if side == 1 else XW - 1
                remote(rly.at[m], xr.at[1 - side, chunk(c)], rf_sem.at[m], xr_sem.at[1 - side, c], "sx", dest).wait_send()

    def par_copy(c):
        return pltpu.make_async_remote_copy(
            snap.at[chunk(c)], peer.at[chunk(c)], ps_sem.at[c], pr_sem.at[c],
            device_id={"par": 1 - par}, device_id_type=MESH,
        )

    col = lax.rem(sx, XW)
    outer = (col == 0) | (col == XW - 1)
    pair = jnp.where(lax.rem(sx, 2) == 0, sx + 1, sx - 1)

    def detours(c):
        i = (c - NC // 2) // 2
        return (c >= NC // 2) & (lax.rem(c, 2) == 0) & (i < DETOUR), i

    def par_start(c):
        takes, i = detours(c)
        takes = takes & outer

        @pl.when(takes)
        def _():
            pltpu.make_async_remote_copy(
                snap.at[chunk(c)], rlp.at[i], ps_sem.at[c], dr_sem.at[i],
                device_id={"sx": pair, "par": 1 - par}, device_id_type=MESH,
            ).start()

        @pl.when(jnp.logical_not(takes))
        def _():
            par_copy(c).start()

    def pass_copy(c, i):
        return remote(rlp.at[i], peer.at[chunk(c)], ds_sem.at[i], pr_sem.at[c], "sx", pair)

    def par_pass(c):
        due, i = detours(c)

        @pl.when(due & jnp.logical_not(outer))
        def _():
            remote(rlp.at[i], rlp.at[i], ds_sem.at[i], dr_sem.at[i], "sx", pair).wait_recv()
            pass_copy(c, i).start()

    @pl.loop(0, NC)
    def _(c):
        for cp in load(c):
            cp.start()

    psi_load = pltpu.make_async_copy(psi_hbm, psi, aux_sem.at[0])
    omega_load = pltpu.make_async_copy(omega_hbm, omega_ref, aux_sem.at[1])
    psi_load.start()
    omega_load.start()

    barrier = pltpu.get_barrier_semaphore()
    for d in range(1, nsx):
        pl.semaphore_signal(barrier, inc=1, device_id={"sx": lax.rem(sx + d, nsx)}, device_id_type=MESH)
    for d in range(1, nsy):
        pl.semaphore_signal(barrier, inc=1, device_id={"sy": lax.rem(sy + d, nsy)}, device_id_type=MESH)
    pl.semaphore_signal(barrier, inc=1, device_id={"par": 1 - par}, device_id_type=MESH)
    pl.semaphore_signal(barrier, inc=1, device_id={"sx": pair, "par": 1 - par}, device_id_type=MESH)

    for side in (0, 1):
        @pl.when(jnp.logical_not(has["sx", side]))
        def _():
            @pl.loop(0, S)
            def _(s):
                xr[side, s] = jnp.zeros(xr.shape[2:], BF16)

        @pl.when(jnp.logical_not(has["sy", side]))
        def _():
            @pl.loop(0, S)
            def _(s):
                yr[side, s] = jnp.zeros(yr.shape[2:], BF16)

    row8 = lax.broadcasted_iota(jnp.int32, (1, 8, Z), 1)
    low4 = row8 < 4
    yrow = lax.broadcasted_iota(jnp.int32, (1, Y + 2 * H, Z), 1)
    lane = lax.broadcasted_iota(jnp.int32, (1, Y + 2 * H, Z), 2)
    cut = ((yrow == H - 1) & (sy == 0)) | ((yrow == H + Y - 1) & (sy == nsy - 1))
    ymask = jnp.where(cut, 0.0, 1.0).astype(F32)

    pl.semaphore_wait(barrier, nsx + nsy)

    def x_edges(c):
        for cp in load(c):
            cp.wait()

        @pl.loop(0, CHUNK)
        def _(j):
            s = c * CHUNK + j
            for side, at in ((0, 0), (1, X - H)):
                xs[side, s, 0:H] = u_in[s, at:at + H].astype(BF16)
                xs[side, s, H:2 * H] = k_in[s, at:at + H].astype(BF16)

        for side in (0, 1):
            turn = detour(side, c)[0]

            @pl.when(has["sx", side] & turn)
            def _():
                to_relay(side, c).start()

            @pl.when(has["sx", side] & jnp.logical_not(turn))
            def _():
                halo("sx", side, c).start()

    @pl.loop(0, AHEAD)
    def _(c):
        x_edges(c)

    def half(s, x0, n, tile):
        rows = slice(8 * tile, 8 * tile + 8)
        if x0 < H:
            v = xr[0, s].astype(F32)
            return v[0:H, rows], v[H:2 * H, rows]
        if x0 >= H + X:
            v = xr[1, s].astype(F32)
            return v[0:H, rows], v[H:2 * H, rows]
        return u_in[s, x0 - H:x0 - H + n, rows], k_in[s, x0 - H:x0 - H + n, rows]

    groups = [(x0, H) for x0 in range(0, XE, H)]

    def y_edges(c):
        for side in (0, 1):
            @pl.when(has["sx", side])
            def _():
                halo_recv("sx", side, c).wait_recv()

        @pl.loop(0, CHUNK)
        def _(j):
            s = c * CHUNK + j
            for x0, n in groups:
                u0, k0 = half(s, x0, n, 0)
                u1, k1 = half(s, x0, n, 1)
                p = jnp.where(low4, k0, pltpu.roll(u0, 4, 1))
                q = jnp.where(low4, pltpu.roll(u1, 4, 1), k1)
                ys[0, s, x0 // 2:x0 // 2 + n // 2] = p.reshape(n // 2, 16, Z).astype(BF16)
                ys[1, s, x0 // 2:x0 // 2 + n // 2] = q.reshape(n // 2, 16, Z).astype(BF16)

        for side in (0, 1):
            @pl.when(has["sy", side])
            def _():
                halo("sy", side, c).start()

    def zshift(v, by):
        return pltpu.roll(v, by % Z, 2)

    def yshift(v, by):
        return pltpu.roll(v, by % v.shape[1], 1)

    def sample(s):
        for x0, n in groups:
            u0, k0 = half(s, x0, n, 0)
            u1, k1 = half(s, x0, n, 1)
            lo = yr[0, s, x0 // 2:x0 // 2 + n // 2].astype(F32).reshape(n, 8, Z)
            hi = yr[1, s, x0 // 2:x0 // 2 + n // 2].astype(F32).reshape(n, 8, Z)
            a, b = pltpu.roll(u0, 4, 1), pltpu.roll(u1, 4, 1)
            ua[x0:x0 + n, 0:8] = jnp.where(low4, lo, a)
            ua[x0:x0 + n, 8:16] = jnp.where(low4, a, b)
            ua[x0:x0 + n, 16:24] = jnp.where(low4, b, hi)
            a, b = pltpu.roll(k0, 4, 1), pltpu.roll(k1, 4, 1)
            kk[x0:x0 + n, 0:8] = jnp.where(low4, pltpu.roll(lo, 4, 1), a) * 0.08
            kk[x0:x0 + n, 8:16] = jnp.where(low4, a, b) * 0.08
            kk[x0:x0 + n, 16:24] = jnp.where(low4, b, pltpu.roll(hi, 4, 1)) * 0.08

        cx[0:1] = kk[0:1] + kk[1:2]

        def faces(i, _):
            x = pl.ds(1 + 2 * i, 2)
            k = kk[x]
            fx = k + kk[pl.ds(2 + 2 * i, 2)]
            bx = k + kk[pl.ds(2 * i, 2)]
            fy = k + yshift(k, -1)
            by = yshift(fy, 1)
            fz = k + jnp.where(lane < Z - 1, zshift(k, -1), 0.0)
            bz = k + jnp.where(lane > 0, zshift(k, 1), 0.0)
            dd[x] = 1.0 - (((fx + bx) + (fy + by)) + (fz + bz))
            cx[x] = fx
            cy[x] = fy * ymask
            cz[x] = jnp.where(lane < Z - 1, fz, 0.0)
            return 0

        lax.fori_loop(0, (XE - 2) // 2, faces, 0, unroll=True)

        @pl.when(sx == 0)
        def _():
            cx[H - 1:H] = jnp.zeros((1, Y + 2 * H, Z), F32)

        @pl.when(sx == nsx - 1)
        def _():
            cx[H + X - 1:H + X] = jnp.zeros((1, Y + 2 * H, Z), F32)

        def stencil(src, x0):
            x = pl.ds(x0, 2)
            u = src[x]
            y_c, z_c = cy[x], cz[x]
            out = dd[x] * u
            out += cx[x] * src[pl.ds(x0 + 1, 2)] + cx[pl.ds(x0 - 1, 2)] * src[pl.ds(x0 - 1, 2)]
            out += y_c * yshift(u, -1) + yshift(y_c * u, 1)
            out += z_c * zshift(u, -1) + zshift(z_c * u, 1)
            return out

        src, dst = ua, ub
        for step in range(STEPS - 1):
            first = 1 + step

            def advance(i, _, src=src, dst=dst, first=first):
                dst[pl.ds(first + 2 * i, 2)] = stencil(src, first + 2 * i)
                return 0

            lax.fori_loop(0, (XE - 2 * first) // 2, advance, 0, unroll=True)
            src, dst = dst, src

        def last(i, _, src=src):
            v = stencil(src, H + 2 * i)
            v0, v1, v2 = (pltpu.roll(v[:, 8 * t:8 * t + 8], 4, 1) for t in range(3))
            a, b = jnp.where(low4, v0, v1), jnp.where(low4, v1, v2)
            o = jnp.concatenate([a, b], axis=1)
            u_in[s, pl.ds(2 * i, 2)] = o
            snap[s, pl.ds(2 * i, 2)] = o.astype(BF16)
            return 0

        lax.fori_loop(0, X // 2, last, 0, unroll=True)

    y_edges(0)
    relay(jnp.int32(1))
    relay(jnp.int32(2))
    y_edges(1)

    SB, RB = 16, 16

    def corange(sb):
        @pl.loop(0, R // RB)
        def _(rb):
            val = None
            for x in range(0, X, 2):
                left = jnp.concatenate([psi[pl.ds(rb * RB, RB), x + d].reshape(RB * Y, Z) for d in range(2)], axis=1)
                right = jnp.concatenate([snap[pl.ds(sb * SB, SB), x + d].reshape(SB * Y, Z) for d in range(2)], axis=1)
                term = lax.dot_general(left, right, (((1,), (1,)), ((), ())), preferred_element_type=F32)
                val = term if val is None else val + term
            w_r = lax.rem(lax.broadcasted_iota(jnp.int32, (RB * Y, SB * Y), 0), Y)
            w_c = lax.rem(lax.broadcasted_iota(jnp.int32, (RB * Y, SB * Y), 1), Y)
            val = jnp.where(w_r == w_c, val, 0.0).reshape(RB, Y, SB * Y)
            red[sb, pl.ds(rb * RB, RB)] = jnp.sum(val, axis=1)

    psi_load.wait()

    @pl.loop(0, NC)
    def _(c):
        for sb in range(S // SB - 1):
            @pl.when(c == (sb + 1) * SB // CHUNK)
            def _():
                corange(sb)

        @pl.when(c + AHEAD < NC)
        def _():
            x_edges(c + AHEAD)

        upto = jnp.minimum(2 * c + 4, c + 8)

        @pl.loop(jnp.minimum(2 * c + 2, c + 8 - 1) + 1, upto + 1)
        def _(i):
            relay(i)

        @pl.when(c + 2 < NC)
        def _():
            y_edges(c + 2)

        for side in (0, 1):
            @pl.when(has["sy", side])
            def _():
                halo_recv("sy", side, c).wait_recv()

        @pl.loop(0, CHUNK)
        def _(j):
            sample(c * CHUNK + j)

        @pl.when(c < NC - HELD)
        def _():
            par_start(c)

        par_pass(c - LAG)

    corange(S // SB - 1)

    g_r = lax.broadcasted_iota(jnp.int32, (SB, SB * Y), 0)
    g_c = lax.broadcasted_iota(jnp.int32, (SB, SB * Y), 1) // Y
    group = jnp.where(g_r == g_c, 1.0, 0.0).astype(F32)
    part[...] = jnp.concatenate([
        lax.dot_general(group, red[q], (((1,), (1,)), ((), ())), preferred_element_type=F32, precision=lax.Precision.HIGHEST)
        for q in range(S // SB)], axis=1)

    def gather(axis, d, src, dst, ssem, rsem):
        n = dst.shape[0]
        return remote(src, dst.at[pos[axis]], ssem.at[d], rsem.at[d], axis, lax.rem(pos[axis] + d, n))

    def gather_recv(axis, d, src, dst, ssem, rsem):
        n = dst.shape[0]
        return remote(src, dst.at[lax.rem(pos[axis] + n - d, n)], ssem.at[d], rsem.at[d], axis, lax.rem(pos[axis] + d, n))

    for d in range(1, nsx):
        gather("sx", d, part, gat1, a1s_sem, a1r_sem).start()

    @pl.loop(NC - HELD, NC)
    def _(c):
        par_start(c)

    @pl.loop(NC - LAG, NC)
    def _(c):
        par_pass(c)

    omega_load.wait()
    i_r = lax.broadcasted_iota(jnp.int32, (RD * Y, R), 0) // Y
    i_j = lax.broadcasted_iota(jnp.int32, (RD * Y, R), 1)
    pick = jnp.where(i_j == i_r + par * RD, 1.0, 0.0).astype(BF16)
    cols = lax.dot_general(pick, omega_ref[...], (((1,), (1,)), ((), ())), preferred_element_type=F32).astype(BF16)
    total = omega_ref.shape[0]
    WB = 256

    @pl.loop(0, total * Y // WB)
    def _(b):
        e_s = lax.broadcasted_iota(jnp.int32, (total, WB), 0)
        e_c = lax.broadcasted_iota(jnp.int32, (total, WB), 1) + b * WB
        spread = jnp.where(e_s == lax.rem(e_c // Y + par * S, total), 1.0, 0.0).astype(BF16)
        wide = jnp.dot(cols, spread, preferred_element_type=F32)
        w_r = lax.rem(lax.broadcasted_iota(jnp.int32, (RD * Y, WB), 0), Y)
        w_c = lax.rem(lax.broadcasted_iota(jnp.int32, (RD * Y, WB), 1), Y)
        w_ref[:, pl.ds(pl.multiple_of(b * WB, WB), WB)] = jnp.where(w_r == w_c, wide, 0.0).astype(BF16)


    def range_part(x0, weights, source, lo, n):
        right = jnp.concatenate([source[lo:lo + n, x0 + d].reshape(n * Y, Z) for d in range(2)], axis=1)
        return jnp.dot(weights, right, preferred_element_type=F32)

    for x0 in range(0, X, 2):
        t = range_part(x0, w_ref[:, 0:S * Y], snap, 0, S)
        for d in range(2):
            acc[x0 + d] = t[:, d * Z:(d + 1) * Z]

    gat1[pl.ds(sx, 1)] = part[...][None]
    for d in range(1, nsx):
        gather("sx", d, part, gat1, a1s_sem, a1r_sem).wait_send()
        gather_recv("sx", d, part, gat1, a1s_sem, a1r_sem).wait_recv()
    tot = gat1[0]
    for i in range(1, nsx):
        tot += gat1[i]
    part2[...] = tot
    for d in range(1, nsy):
        gather("sy", d, part2, gat2, a2s_sem, a2r_sem).start()

    HALF = S // 2
    for c in range(NC // 2):
        par_copy(c).wait_recv()
    for x0 in range(0, X, 2):
        t = range_part(x0, w_ref[:, S * Y:(S + HALF) * Y], peer, 0, HALF)
        for d in range(2):
            acc[x0 + d] = acc[x0 + d] + t[:, d * Z:(d + 1) * Z]

    gat2[pl.ds(sy, 1)] = part2[...][None]
    for d in range(1, nsy):
        gather("sy", d, part2, gat2, a2s_sem, a2r_sem).wait_send()
        gather_recv("sy", d, part2, gat2, a2s_sem, a2r_sem).wait_recv()
    tot = gat2[0]
    for i in range(1, nsy):
        tot += gat2[i]
    for q in range(S // SB):
        cor_ref[q * SB:(q + 1) * SB] = tot[:, q * R:(q + 1) * R]

    for c in range(NC // 2, NC):
        par_copy(c).wait_recv()

    for x0 in range(0, X, 2):
        t = range_part(x0, w_ref[:, (S + HALF) * Y:2 * S * Y], peer, HALF, HALF)
        for d in range(2):
            acc[x0 + d] = acc[x0 + d] + t[:, d * Z:(d + 1) * Z]

    @pl.loop(0, NC)
    def _(c):
        for side in (0, 1):
            for axis in ("sx", "sy"):
                @pl.when(has[axis, side])
                def _():
                    halo(axis, side, c).wait_send()
        relay_done(c)
        due, i = detours(c)

        @pl.when(due & jnp.logical_not(outer))
        def _():
            pass_copy(c, i).wait_send()

        par_copy(c).wait_send()


def store(fin_ref, acc_ref, cor_ref, prev_hbm, cprev_ref, fin_hbm, rng_hbm, cor_out, prev, rng, sem):
    RD, X, Y, Z = prev.shape
    N = PIECES
    n, m = RD // N, fin_ref.shape[0] // N
    loads = [pltpu.make_async_copy(prev_hbm.at[pl.ds(p * n, n)], prev.at[pl.ds(p * n, n)], sem.at[0, p]) for p in range(N)]
    fins = [pltpu.make_async_copy(fin_ref.at[pl.ds(p * m, m)], fin_hbm.at[pl.ds(p * m, m)], sem.at[1, p]) for p in range(N)]
    outs = [pltpu.make_async_copy(rng.at[pl.ds(p * n, n)], rng_hbm.at[pl.ds(p * n, n)], sem.at[2, p]) for p in range(N)]
    for cp in loads + fins:
        cp.start()
    cor_out[...] = cprev_ref[...] + cor_ref[...]
    for p in range(N):
        loads[p].wait()

        def add(x, _, p=p):
            new = acc_ref[x, p * n * Y:(p + 1) * n * Y].reshape(n, Y, Z)
            rng[p * n:(p + 1) * n, x] = (prev[p * n:(p + 1) * n, x].astype(F32) + new).astype(BF16)
            return 0

        lax.fori_loop(0, X, add, 0, unroll=True)
        outs[p].start()
    for cp in fins + outs:
        cp.wait()


def per_device(sizes, initial_state, conductivity, omega, psi, range_prev, corange_prev):
    S, X, Y, Z = initial_state.shape
    R, RD = psi.shape[0], range_prev.shape[0]
    nsx, nsy = sizes
    NC = S // CHUNK
    E = (X + 2 * H, Y + 2 * H, Z)
    dma = pltpu.SemaphoreType.DMA
    scratch = [
        pltpu.VMEM((S, X, Y, Z), F32),
        pltpu.VMEM((2, S, 2 * H, Y, Z), BF16),
        pltpu.VMEM((2, S, 2 * H, Y, Z), BF16),
        pltpu.VMEM((NC // 2, CHUNK, 2 * H, Y, Z), BF16),
        pltpu.VMEM((DETOUR, CHUNK, X, Y, Z), BF16),
        pltpu.VMEM((2, S, E[0] // 2, 16, Z), BF16),
        pltpu.VMEM((2, S, E[0] // 2, 16, Z), BF16),
        pltpu.VMEM((S, X, Y, Z), BF16),
        pltpu.VMEM((S, X, Y, Z), BF16),
        pltpu.VMEM((R, X, Y, Z), BF16),
        pltpu.VMEM(omega.shape, BF16),
        pltpu.VMEM((RD * Y, 2 * S * Y), BF16),
        pltpu.VMEM((S // 16, R, 16 * Y), F32),
        pltpu.VMEM((R * S // Z, Z), F32),
        pltpu.VMEM((nsx, R * S // Z, Z), F32),
        pltpu.VMEM((R * S // Z, Z), F32),
        pltpu.VMEM((nsy, R * S // Z, Z), F32),
    ] + [pltpu.VMEM(E, F32)] * 7 + [
        dma((2, NC)), dma((2,)), dma((2, NC)), dma((2, NC)), dma((NC // 2,)), dma((NC // 2,)),
        dma((2, NC)), dma((2, NC)), dma((NC,)), dma((NC,)), dma((DETOUR,)), dma((DETOUR,)),
        dma((nsx,)), dma((nsx,)), dma((nsy,)), dma((nsy,)),
    ]
    any_ = pl.BlockSpec(memory_space=pl.ANY)
    hbm = pl.BlockSpec(memory_space=pltpu.HBM)
    vmem = pl.BlockSpec(memory_space=pltpu.VMEM)
    final, sketch, corange = pl.pallas_call(
        kernel,
        out_shape=(
            jax.ShapeDtypeStruct(initial_state.shape, F32),
            jax.ShapeDtypeStruct((X, RD * Y, Z), F32),
            jax.ShapeDtypeStruct(corange_prev.shape[::-1], F32),
        ),
        in_specs=[hbm, hbm, hbm, hbm],
        out_specs=(vmem, vmem, vmem),
        scratch_shapes=scratch,
        compiler_params=pltpu.CompilerParams(
            collective_id=0, has_side_effects=True, vmem_limit_bytes=VMEM_MIB * 2**20
        ),
    )(initial_state, conductivity, omega, psi)
    final, sketch, corange = pl.pallas_call(
        store,
        out_shape=(
            jax.ShapeDtypeStruct(initial_state.shape, F32),
            jax.ShapeDtypeStruct(range_prev.shape, BF16),
            jax.ShapeDtypeStruct(corange_prev.shape[::-1], F32),
        ),
        in_specs=[vmem, vmem, vmem, any_, vmem],
        out_specs=(any_, any_, vmem),
        scratch_shapes=[pltpu.VMEM(range_prev.shape, BF16), pltpu.VMEM(range_prev.shape, BF16), dma((3, PIECES))],
        compiler_params=pltpu.CompilerParams(vmem_limit_bytes=16 * 2**20),
    )(final, sketch, corange, range_prev, corange_prev.T)
    return final, sketch, corange.T


def solution(mesh):
    in_specs = (
        P("par", "sx", "sy", None),
        P("par", "sx", "sy", None),
        P(),
        P(None, "sx", "sy", None),
        P("par", "sx", "sy", None),
        P(None, "par"),
    )
    out_specs = (P("par", "sx", "sy", None), P("par", "sx", "sy", None), P(None, "par"))
    sizes = (mesh.shape["sx"], mesh.shape["sy"])
    return jax.shard_map(
        functools.partial(per_device, sizes), mesh=mesh, in_specs=in_specs, out_specs=out_specs, check_vma=False
    )
```

```python
import functools

import jax
import jax.numpy as jnp
from jax import lax
from jax.experimental import pallas as pl
from jax.experimental.pallas import tpu as pltpu
from jax.sharding import PartitionSpec as P

STEPS = 4
H = STEPS
MESH = pl.DeviceIdType.MESH
F32 = jnp.float32
BF16 = jnp.bfloat16
CHUNK = 2
AHEAD = 16
HELD = 4
VMEM_MIB = 44
PIECES = 4
DETOUR = 1
LAG = 3


def kernel(
    u_hbm, k_hbm, omega_hbm, psi_hbm,
    u_in, acc, cor_ref,
    k_in, xs, xr, rly, rlp, ys, yr, snap, peer, psi, omega_ref, w_ref, red, part, gat1, part2, gat2,
    ua, ub, kk, cx, cy, cz, dd,
    load_sem, aux_sem, xs_sem, xr_sem, ry_sem, rf_sem, ys_sem, yr_sem, ps_sem, pr_sem, ds_sem, dr_sem,
    a1s_sem, a1r_sem, a2s_sem, a2r_sem,
):
    S, X, Y, Z = u_in.shape
    NC = S // CHUNK
    XE = X + 2 * H
    R = psi.shape[0]
    RD = acc.shape[1] // Y
    sx, sy, par = lax.axis_index("sx"), lax.axis_index("sy"), lax.axis_index("par")
    nsx, nsy = gat1.shape[0], gat2.shape[0]
    has = {("sx", 0): sx > 0, ("sx", 1): sx < nsx - 1, ("sy", 0): sy > 0, ("sy", 1): sy < nsy - 1}
    pos = {"sx": sx, "sy": sy}

    def chunk(c):
        return pl.ds(c * CHUNK, CHUNK)

    def load(c):
        return (
            pltpu.make_async_copy(u_hbm.at[chunk(c)], u_in.at[chunk(c)], load_sem.at[0, c]),
            pltpu.make_async_copy(k_hbm.at[chunk(c)], k_in.at[chunk(c)], load_sem.at[1, c]),
        )

    XW = nsx // 2

    def remote(src, dst, ssem, rsem, axis, other):
        return pltpu.make_async_remote_copy(src, dst, ssem, rsem, device_id={axis: other}, device_id_type=MESH)

    def beside(axis, side):
        n = nsx if axis == "sx" else nsy
        return jnp.maximum(pos[axis] - 1, 0) if side == 0 else jnp.minimum(pos[axis] + 1, n - 1)

    def halo(axis, side, c):
        send, recv, ssem, rsem = (xs, xr, xs_sem, xr_sem) if axis == "sx" else (ys, yr, ys_sem, yr_sem)
        return remote(send.at[side, chunk(c)], recv.at[1 - side, chunk(c)], ssem.at[side, c], rsem.at[1 - side, c],
                      axis, beside(axis, side))

    def halo_recv(axis, side, c):
        send, recv, ssem, rsem = (xs, xr, xs_sem, xr_sem) if axis == "sx" else (ys, yr, ys_sem, yr_sem)
        return remote(send.at[side, chunk(c)], recv.at[side, chunk(c)], ssem.at[side, c], rsem.at[side, c],
                      axis, beside(axis, side))

    def detour(side, c):
        q = lax.rem(c, 2) * (XW - 1)
        at_seam = (sx == XW - 1) if side == 1 else (sx == XW)
        via = XW + q if side == 1 else XW - 1 - q
        return at_seam & (q != 0), via, c // 2

    def to_relay(side, c):
        _, via, m = detour(side, c)
        return remote(xs.at[side, chunk(c)], rly.at[m], xs_sem.at[side, c], ry_sem.at[m], "sx", via)

    def relay(c):
        q = lax.rem(c, 2) * (XW - 1)
        m = c // 2
        for side in (0, 1):
            mine = ((sx == XW + q) if side == 1 else (sx == XW - 1 - q)) & (q != 0)

            @pl.when(mine & (c < NC))
            def _():
                dest = XW if side == 1 else XW - 1
                cp = remote(rly.at[m], xr.at[1 - side, chunk(c)], rf_sem.at[m], xr_sem.at[1 - side, c], "sx", dest)
                remote(rly.at[m], rly.at[m], rf_sem.at[m], ry_sem.at[m], "sx", dest).wait_recv()
                cp.start()

    def relay_done(c):
        q = lax.rem(c, 2) * (XW - 1)
        m = c // 2
        for side in (0, 1):
            mine = ((sx == XW + q) if side == 1 else (sx == XW - 1 - q)) & (q != 0)

            @pl.when(mine)
            def _():
                dest = XW if side == 1 else XW - 1
                remote(rly.at[m], xr.at[1 - side, chunk(c)], rf_sem.at[m], xr_sem.at[1 - side, c], "sx", dest).wait_send()

    def par_copy(c):
        return pltpu.make_async_remote_copy(
            snap.at[chunk(c)], peer.at[chunk(c)], ps_sem.at[c], pr_sem.at[c],
            device_id={"par": 1 - par}, device_id_type=MESH,
        )

    col = lax.rem(sx, XW)
    outer = (col == 0) | (col == XW - 1)
    pair = jnp.where(lax.rem(sx, 2) == 0, sx + 1, sx - 1)

    def detours(c):
        i = (c - NC // 2) // 2
        return (c >= NC // 2) & (lax.rem(c, 2) == 0) & (i < DETOUR), i

    def par_start(c):
        takes, i = detours(c)
        takes = takes & outer

        @pl.when(takes)
        def _():
            pltpu.make_async_remote_copy(
                snap.at[chunk(c)], rlp.at[i], ps_sem.at[c], dr_sem.at[i],
                device_id={"sx": pair, "par": 1 - par}, device_id_type=MESH,
            ).start()

        @pl.when(jnp.logical_not(takes))
        def _():
            par_copy(c).start()

    def pass_copy(c, i):
        return remote(rlp.at[i], peer.at[chunk(c)], ds_sem.at[i], pr_sem.at[c], "sx", pair)

    def par_pass(c):
        due, i = detours(c)

        @pl.when(due & jnp.logical_not(outer))
        def _():
            remote(rlp.at[i], rlp.at[i], ds_sem.at[i], dr_sem.at[i], "sx", pair).wait_recv()
            pass_copy(c, i).start()

    @pl.loop(0, NC)
    def _(c):
        for cp in load(c):
            cp.start()

    psi_load = pltpu.make_async_copy(psi_hbm, psi, aux_sem.at[0])
    omega_load = pltpu.make_async_copy(omega_hbm, omega_ref, aux_sem.at[1])
    psi_load.start()
    omega_load.start()

    barrier = pltpu.get_barrier_semaphore()
    for d in range(1, nsx):
        pl.semaphore_signal(barrier, inc=1, device_id={"sx": lax.rem(sx + d, nsx)}, device_id_type=MESH)
    for d in range(1, nsy):
        pl.semaphore_signal(barrier, inc=1, device_id={"sy": lax.rem(sy + d, nsy)}, device_id_type=MESH)
    pl.semaphore_signal(barrier, inc=1, device_id={"par": 1 - par}, device_id_type=MESH)
    pl.semaphore_signal(barrier, inc=1, device_id={"sx": pair, "par": 1 - par}, device_id_type=MESH)

    for side in (0, 1):
        @pl.when(jnp.logical_not(has["sx", side]))
        def _():
            @pl.loop(0, S)
            def _(s):
                xr[side, s] = jnp.zeros(xr.shape[2:], BF16)

        @pl.when(jnp.logical_not(has["sy", side]))
        def _():
            @pl.loop(0, S)
            def _(s):
                yr[side, s] = jnp.zeros(yr.shape[2:], BF16)

    row8 = lax.broadcasted_iota(jnp.int32, (1, 8, Z), 1)
    low4 = row8 < 4
    yrow = lax.broadcasted_iota(jnp.int32, (1, Y + 2 * H, Z), 1)
    lane = lax.broadcasted_iota(jnp.int32, (1, Y + 2 * H, Z), 2)
    cut = ((yrow == H - 1) & (sy == 0)) | ((yrow == H + Y - 1) & (sy == nsy - 1))
    ymask = jnp.where(cut, 0.0, 1.0).astype(F32)

    pl.semaphore_wait(barrier, nsx + nsy)

    def x_edges(c):
        for cp in load(c):
            cp.wait()

        @pl.loop(0, CHUNK)
        def _(j):
            s = c * CHUNK + j
            for side, at in ((0, 0), (1, X - H)):
                xs[side, s, 0:H] = u_in[s, at:at + H].astype(BF16)
                xs[side, s, H:2 * H] = k_in[s, at:at + H].astype(BF16)

        for side in (0, 1):
            turn = detour(side, c)[0]

            @pl.when(has["sx", side] & turn)
            def _():
                to_relay(side, c).start()

            @pl.when(has["sx", side] & jnp.logical_not(turn))
            def _():
                halo("sx", side, c).start()

    @pl.loop(0, AHEAD)
    def _(c):
        x_edges(c)

    def half(s, x0, n, tile):
        rows = slice(8 * tile, 8 * tile + 8)
        if x0 < H:
            v = xr[0, s].astype(F32)
            return v[0:H, rows], v[H:2 * H, rows]
        if x0 >= H + X:
            v = xr[1, s].astype(F32)
            return v[0:H, rows], v[H:2 * H, rows]
        return u_in[s, x0 - H:x0 - H + n, rows], k_in[s, x0 - H:x0 - H + n, rows]

    groups = [(x0, H) for x0 in range(0, XE, H)]

    def y_edges(c):
        for side in (0, 1):
            @pl.when(has["sx", side])
            def _():
                halo_recv("sx", side, c).wait_recv()

        @pl.loop(0, CHUNK)
        def _(j):
            s = c * CHUNK + j
            for x0, n in groups:
                u0, k0 = half(s, x0, n, 0)
                u1, k1 = half(s, x0, n, 1)
                p = jnp.where(low4, k0, pltpu.roll(u0, 4, 1))
                q = jnp.where(low4, pltpu.roll(u1, 4, 1), k1)
                ys[0, s, x0 // 2:x0 // 2 + n // 2] = p.reshape(n // 2, 16, Z).astype(BF16)
                ys[1, s, x0 // 2:x0 // 2 + n // 2] = q.reshape(n // 2, 16, Z).astype(BF16)

        for side in (0, 1):
            @pl.when(has["sy", side])
            def _():
                halo("sy", side, c).start()

    def zshift(v, by):
        return pltpu.roll(v, by % Z, 2)

    def yshift(v, by):
        return pltpu.roll(v, by % v.shape[1], 1)

    def sample(s):
        for x0, n in groups:
            u0, k0 = half(s, x0, n, 0)
            u1, k1 = half(s, x0, n, 1)
            lo = yr[0, s, x0 // 2:x0 // 2 + n // 2].astype(F32).reshape(n, 8, Z)
            hi = yr[1, s, x0 // 2:x0 // 2 + n // 2].astype(F32).reshape(n, 8, Z)
            a, b = pltpu.roll(u0, 4, 1), pltpu.roll(u1, 4, 1)
            ua[x0:x0 + n, 0:8] = jnp.where(low4, lo, a)
            ua[x0:x0 + n, 8:16] = jnp.where(low4, a, b)
            ua[x0:x0 + n, 16:24] = jnp.where(low4, b, hi)
            a, b = pltpu.roll(k0, 4, 1), pltpu.roll(k1, 4, 1)
            kk[x0:x0 + n, 0:8] = jnp.where(low4, pltpu.roll(lo, 4, 1), a) * 0.08
            kk[x0:x0 + n, 8:16] = jnp.where(low4, a, b) * 0.08
            kk[x0:x0 + n, 16:24] = jnp.where(low4, b, pltpu.roll(hi, 4, 1)) * 0.08

        cx[0:1] = kk[0:1] + kk[1:2]

        def faces(i, _):
            x = pl.ds(1 + 2 * i, 2)
            k = kk[x]
            fx = k + kk[pl.ds(2 + 2 * i, 2)]
            bx = k + kk[pl.ds(2 * i, 2)]
            fy = k + yshift(k, -1)
            by = yshift(fy, 1)
            fz = k + jnp.where(lane < Z - 1, zshift(k, -1), 0.0)
            bz = k + jnp.where(lane > 0, zshift(k, 1), 0.0)
            dd[x] = 1.0 - (((fx + bx) + (fy + by)) + (fz + bz))
            cx[x] = fx
            cy[x] = fy * ymask
            cz[x] = jnp.where(lane < Z - 1, fz, 0.0)
            return 0

        lax.fori_loop(0, (XE - 2) // 2, faces, 0, unroll=True)

        @pl.when(sx == 0)
        def _():
            cx[H - 1:H] = jnp.zeros((1, Y + 2 * H, Z), F32)

        @pl.when(sx == nsx - 1)
        def _():
            cx[H + X - 1:H + X] = jnp.zeros((1, Y + 2 * H, Z), F32)

        def stencil(src, x0):
            x = pl.ds(x0, 2)
            u = src[x]
            y_c, z_c = cy[x], cz[x]
            out = dd[x] * u
            out += cx[x] * src[pl.ds(x0 + 1, 2)] + cx[pl.ds(x0 - 1, 2)] * src[pl.ds(x0 - 1, 2)]
            out += y_c * yshift(u, -1) + yshift(y_c * u, 1)
            out += z_c * zshift(u, -1) + zshift(z_c * u, 1)
            return out

        src, dst = ua, ub
        for step in range(STEPS - 1):
            first = 1 + step

            def advance(i, _, src=src, dst=dst, first=first):
                dst[pl.ds(first + 2 * i, 2)] = stencil(src, first + 2 * i)
                return 0

            lax.fori_loop(0, (XE - 2 * first) // 2, advance, 0, unroll=True)
            src, dst = dst, src

        def last(i, _, src=src):
            v = stencil(src, H + 2 * i)
            v0, v1, v2 = (pltpu.roll(v[:, 8 * t:8 * t + 8], 4, 1) for t in range(3))
            a, b = jnp.where(low4, v0, v1), jnp.where(low4, v1, v2)
            o = jnp.concatenate([a, b], axis=1)
            u_in[s, pl.ds(2 * i, 2)] = o
            snap[s, pl.ds(2 * i, 2)] = o.astype(BF16)
            return 0

        lax.fori_loop(0, X // 2, last, 0, unroll=True)

    y_edges(0)
    relay(jnp.int32(1))
    relay(jnp.int32(2))
    y_edges(1)

    SB, RB = 16, 16

    def corange(sb):
        @pl.loop(0, R // RB)
        def _(rb):
            val = None
            for x in range(0, X, 2):
                left = jnp.concatenate([psi[pl.ds(rb * RB, RB), x + d].reshape(RB * Y, Z) for d in range(2)], axis=1)
                right = jnp.concatenate([snap[pl.ds(sb * SB, SB), x + d].reshape(SB * Y, Z) for d in range(2)], axis=1)
                term = lax.dot_general(left, right, (((1,), (1,)), ((), ())), preferred_element_type=F32)
                val = term if val is None else val + term
            w_r = lax.rem(lax.broadcasted_iota(jnp.int32, (RB * Y, SB * Y), 0), Y)
            w_c = lax.rem(lax.broadcasted_iota(jnp.int32, (RB * Y, SB * Y), 1), Y)
            val = jnp.where(w_r == w_c, val, 0.0).reshape(RB, Y, SB * Y)
            red[sb, pl.ds(rb * RB, RB)] = jnp.sum(val, axis=1)

    psi_load.wait()

    @pl.loop(0, NC)
    def _(c):
        for sb in range(S // SB - 1):
            @pl.when(c == (sb + 1) * SB // CHUNK)
            def _():
                corange(sb)

        @pl.when(c + AHEAD < NC)
        def _():
            x_edges(c + AHEAD)

        upto = jnp.minimum(2 * c + 4, c + 8)

        @pl.loop(jnp.minimum(2 * c + 2, c + 8 - 1) + 1, upto + 1)
        def _(i):
            relay(i)

        @pl.when(c + 2 < NC)
        def _():
            y_edges(c + 2)

        for side in (0, 1):
            @pl.when(has["sy", side])
            def _():
                halo_recv("sy", side, c).wait_recv()

        @pl.loop(0, CHUNK)
        def _(j):
            sample(c * CHUNK + j)

        @pl.when(c < NC - HELD)
        def _():
            par_start(c)

        par_pass(c - LAG)

    corange(S // SB - 1)

    g_r = lax.broadcasted_iota(jnp.int32, (SB, SB * Y), 0)
    g_c = lax.broadcasted_iota(jnp.int32, (SB, SB * Y), 1) // Y
    group = jnp.where(g_r == g_c, 1.0, 0.0).astype(F32)
    part[...] = jnp.concatenate([
        lax.dot_general(group, red[q], (((1,), (1,)), ((), ())), preferred_element_type=F32, precision=lax.Precision.HIGHEST)
        for q in range(S // SB)], axis=1)

    def gather(axis, d, src, dst, ssem, rsem):
        n = dst.shape[0]
        return remote(src, dst.at[pos[axis]], ssem.at[d], rsem.at[d], axis, lax.rem(pos[axis] + d, n))

    def gather_recv(axis, d, src, dst, ssem, rsem):
        n = dst.shape[0]
        return remote(src, dst.at[lax.rem(pos[axis] + n - d, n)], ssem.at[d], rsem.at[d], axis, lax.rem(pos[axis] + d, n))

    for d in range(1, nsx):
        gather("sx", d, part, gat1, a1s_sem, a1r_sem).start()

    @pl.loop(NC - HELD, NC)
    def _(c):
        par_start(c)

    @pl.loop(NC - LAG, NC)
    def _(c):
        par_pass(c)

    omega_load.wait()
    i_r = lax.broadcasted_iota(jnp.int32, (RD * Y, R), 0) // Y
    i_j = lax.broadcasted_iota(jnp.int32, (RD * Y, R), 1)
    pick = jnp.where(i_j == i_r + par * RD, 1.0, 0.0).astype(BF16)
    cols = lax.dot_general(pick, omega_ref[...], (((1,), (1,)), ((), ())), preferred_element_type=F32).astype(BF16)
    total = omega_ref.shape[0]
    WB = 256

    @pl.loop(0, total * Y // WB)
    def _(b):
        e_s = lax.broadcasted_iota(jnp.int32, (total, WB), 0)
        e_c = lax.broadcasted_iota(jnp.int32, (total, WB), 1) + b * WB
        spread = jnp.where(e_s == lax.rem(e_c // Y + par * S, total), 1.0, 0.0).astype(BF16)
        wide = jnp.dot(cols, spread, preferred_element_type=F32)
        w_r = lax.rem(lax.broadcasted_iota(jnp.int32, (RD * Y, WB), 0), Y)
        w_c = lax.rem(lax.broadcasted_iota(jnp.int32, (RD * Y, WB), 1), Y)
        w_ref[:, pl.ds(pl.multiple_of(b * WB, WB), WB)] = jnp.where(w_r == w_c, wide, 0.0).astype(BF16)


    def range_part(x0, weights, source, lo, n):
        right = jnp.concatenate([source[lo:lo + n, x0 + d].reshape(n * Y, Z) for d in range(2)], axis=1)
        return jnp.dot(weights, right, preferred_element_type=F32)

    for x0 in range(0, X, 2):
        t = range_part(x0, w_ref[:, 0:S * Y], snap, 0, S)
        for d in range(2):
            acc[x0 + d] = t[:, d * Z:(d + 1) * Z]

    gat1[pl.ds(sx, 1)] = part[...][None]
    for d in range(1, nsx):
        gather("sx", d, part, gat1, a1s_sem, a1r_sem).wait_send()
        gather_recv("sx", d, part, gat1, a1s_sem, a1r_sem).wait_recv()
    tot = gat1[0]
    for i in range(1, nsx):
        tot += gat1[i]
    part2[...] = tot
    for d in range(1, nsy):
        gather("sy", d, part2, gat2, a2s_sem, a2r_sem).start()

    HALF = S // 2
    for c in range(NC // 2):
        par_copy(c).wait_recv()
    for x0 in range(0, X, 2):
        t = range_part(x0, w_ref[:, S * Y:(S + HALF) * Y], peer, 0, HALF)
        for d in range(2):
            acc[x0 + d] = acc[x0 + d] + t[:, d * Z:(d + 1) * Z]

    gat2[pl.ds(sy, 1)] = part2[...][None]
    for d in range(1, nsy):
        gather("sy", d, part2, gat2, a2s_sem, a2r_sem).wait_send()
        gather_recv("sy", d, part2, gat2, a2s_sem, a2r_sem).wait_recv()
    tot = gat2[0]
    for i in range(1, nsy):
        tot += gat2[i]
    for q in range(S // SB):
        cor_ref[q * SB:(q + 1) * SB] = tot[:, q * R:(q + 1) * R]

    for c in range(NC // 2, NC):
        par_copy(c).wait_recv()

    for x0 in range(0, X, 2):
        t = range_part(x0, w_ref[:, (S + HALF) * Y:2 * S * Y], peer, HALF, HALF)
        for d in range(2):
            acc[x0 + d] = acc[x0 + d] + t[:, d * Z:(d + 1) * Z]

    @pl.loop(0, NC)
    def _(c):
        for side in (0, 1):
            for axis in ("sx", "sy"):
                @pl.when(has[axis, side])
                def _():
                    halo(axis, side, c).wait_send()
        relay_done(c)
        due, i = detours(c)

        @pl.when(due & jnp.logical_not(outer))
        def _():
            pass_copy(c, i).wait_send()

        par_copy(c).wait_send()


def store(fin_ref, acc_ref, cor_ref, prev_hbm, cprev_ref, fin_hbm, rng_hbm, cor_out, prev, rng, sem):
    RD, X, Y, Z = prev.shape
    N = PIECES
    n, m = RD // N, fin_ref.shape[0] // N
    loads = [pltpu.make_async_copy(prev_hbm.at[pl.ds(p * n, n)], prev.at[pl.ds(p * n, n)], sem.at[0, p]) for p in range(N)]
    fins = [pltpu.make_async_copy(fin_ref.at[pl.ds(p * m, m)], fin_hbm.at[pl.ds(p * m, m)], sem.at[1, p]) for p in range(N)]
    outs = [pltpu.make_async_copy(rng.at[pl.ds(p * n, n)], rng_hbm.at[pl.ds(p * n, n)], sem.at[2, p]) for p in range(N)]
    for cp in loads + fins:
        cp.start()
    cor_out[...] = cprev_ref[...] + cor_ref[...]
    for p in range(N):
        loads[p].wait()

        def add(x, _, p=p):
            new = acc_ref[x, p * n * Y:(p + 1) * n * Y].reshape(n, Y, Z)
            rng[p * n:(p + 1) * n, x] = (prev[p * n:(p + 1) * n, x].astype(F32) + new).astype(BF16)
            return 0

        lax.fori_loop(0, X, add, 0, unroll=True)
        outs[p].start()
    for cp in fins + outs:
        cp.wait()


def per_device(sizes, initial_state, conductivity, omega, psi, range_prev, corange_prev):
    S, X, Y, Z = initial_state.shape
    R, RD = psi.shape[0], range_prev.shape[0]
    nsx, nsy = sizes
    NC = S // CHUNK
    E = (X + 2 * H, Y + 2 * H, Z)
    dma = pltpu.SemaphoreType.DMA
    scratch = [
        pltpu.VMEM((S, X, Y, Z), F32),
        pltpu.VMEM((2, S, 2 * H, Y, Z), BF16),
        pltpu.VMEM((2, S, 2 * H, Y, Z), BF16),
        pltpu.VMEM((NC // 2, CHUNK, 2 * H, Y, Z), BF16),
        pltpu.VMEM((DETOUR, CHUNK, X, Y, Z), BF16),
        pltpu.VMEM((2, S, E[0] // 2, 16, Z), BF16),
        pltpu.VMEM((2, S, E[0] // 2, 16, Z), BF16),
        pltpu.VMEM((S, X, Y, Z), BF16),
        pltpu.VMEM((S, X, Y, Z), BF16),
        pltpu.VMEM((R, X, Y, Z), BF16),
        pltpu.VMEM(omega.shape, BF16),
        pltpu.VMEM((RD * Y, 2 * S * Y), BF16),
        pltpu.VMEM((S // 16, R, 16 * Y), F32),
        pltpu.VMEM((R * S // Z, Z), F32),
        pltpu.VMEM((nsx, R * S // Z, Z), F32),
        pltpu.VMEM((R * S // Z, Z), F32),
        pltpu.VMEM((nsy, R * S // Z, Z), F32),
    ] + [pltpu.VMEM(E, F32)] * 7 + [
        dma((2, NC)), dma((2,)), dma((2, NC)), dma((2, NC)), dma((NC // 2,)), dma((NC // 2,)),
        dma((2, NC)), dma((2, NC)), dma((NC,)), dma((NC,)), dma((DETOUR,)), dma((DETOUR,)),
        dma((nsx,)), dma((nsx,)), dma((nsy,)), dma((nsy,)),
    ]
    any_ = pl.BlockSpec(memory_space=pl.ANY)
    hbm = pl.BlockSpec(memory_space=pltpu.HBM)
    vmem = pl.BlockSpec(memory_space=pltpu.VMEM)
    final, sketch, corange = pl.pallas_call(
        kernel,
        out_shape=(
            jax.ShapeDtypeStruct(initial_state.shape, F32),
            jax.ShapeDtypeStruct((X, RD * Y, Z), F32),
            jax.ShapeDtypeStruct(corange_prev.shape[::-1], F32),
        ),
        in_specs=[hbm, hbm, hbm, hbm],
        out_specs=(vmem, vmem, vmem),
        scratch_shapes=scratch,
        compiler_params=pltpu.CompilerParams(
            collective_id=0, has_side_effects=True, vmem_limit_bytes=VMEM_MIB * 2**20
        ),
    )(initial_state, conductivity, pltpu.with_memory_space_constraint(omega, pltpu.HBM), psi)
    final, sketch, corange = pl.pallas_call(
        store,
        out_shape=(
            jax.ShapeDtypeStruct(initial_state.shape, F32),
            jax.ShapeDtypeStruct(range_prev.shape, BF16),
            jax.ShapeDtypeStruct(corange_prev.shape[::-1], F32),
        ),
        in_specs=[vmem, vmem, vmem, any_, vmem],
        out_specs=(any_, any_, vmem),
        scratch_shapes=[pltpu.VMEM(range_prev.shape, BF16), pltpu.VMEM(range_prev.shape, BF16), dma((3, PIECES))],
        compiler_params=pltpu.CompilerParams(vmem_limit_bytes=16 * 2**20),
    )(final, sketch, corange, range_prev, corange_prev.T)
    return final, sketch, corange.T


def solution(mesh):
    in_specs = (
        P("par", "sx", "sy", None),
        P("par", "sx", "sy", None),
        P(),
        P(None, "sx", "sy", None),
        P("par", "sx", "sy", None),
        P(None, "par"),
    )
    out_specs = (P("par", "sx", "sy", None), P("par", "sx", "sy", None), P(None, "par"))
    sizes = (mesh.shape["sx"], mesh.shape["sy"])
    return jax.shard_map(
        functools.partial(per_device, sizes), mesh=mesh, in_specs=in_specs, out_specs=out_specs, check_vma=False
    )
```

```python
import functools

import jax
import jax.numpy as jnp
from jax import lax
from jax.experimental import pallas as pl
from jax.experimental.pallas import tpu as pltpu
from jax.sharding import PartitionSpec as P

STEPS = 4
H = STEPS
MESH = pl.DeviceIdType.MESH
F32 = jnp.float32
BF16 = jnp.bfloat16
CHUNK = 2
AHEAD = 16
HELD = 4
VMEM_MIB = 44
PIECES = 4
DETOUR = 1
LAG = 3


def kernel(
    u_hbm, k_hbm, omega_hbm, psi_hbm,
    u_in, acc, cor_ref,
    k_in, xs, xr, rly, rlp, ys, yr, snap, peer, psi, omega_ref, w_ref, red, part, gat1, part2, gat2,
    ua, ub, kk, cx, cy, cz, dd,
    load_sem, aux_sem, xs_sem, xr_sem, ry_sem, rf_sem, ys_sem, yr_sem, ps_sem, pr_sem, ds_sem, dr_sem,
    a1s_sem, a1r_sem, a2s_sem, a2r_sem,
):
    S, X, Y, Z = u_in.shape
    NC = S // CHUNK
    XE = X + 2 * H
    R = psi.shape[0]
    RD = acc.shape[1] // Y
    sx, sy, par = lax.axis_index("sx"), lax.axis_index("sy"), lax.axis_index("par")
    nsx, nsy = gat1.shape[0], gat2.shape[0]
    has = {("sx", 0): sx > 0, ("sx", 1): sx < nsx - 1, ("sy", 0): sy > 0, ("sy", 1): sy < nsy - 1}
    pos = {"sx": sx, "sy": sy}

    def chunk(c):
        return pl.ds(c * CHUNK, CHUNK)

    def load(c):
        return (
            pltpu.make_async_copy(u_hbm.at[chunk(c)], u_in.at[chunk(c)], load_sem.at[0, c]),
            pltpu.make_async_copy(k_hbm.at[chunk(c)], k_in.at[chunk(c)], load_sem.at[1, c]),
        )

    XW = nsx // 2

    def remote(src, dst, ssem, rsem, axis, other):
        return pltpu.make_async_remote_copy(src, dst, ssem, rsem, device_id={axis: other}, device_id_type=MESH)

    def beside(axis, side):
        n = nsx if axis == "sx" else nsy
        return jnp.maximum(pos[axis] - 1, 0) if side == 0 else jnp.minimum(pos[axis] + 1, n - 1)

    def halo(axis, side, c):
        send, recv, ssem, rsem = (xs, xr, xs_sem, xr_sem) if axis == "sx" else (ys, yr, ys_sem, yr_sem)
        return remote(send.at[side, chunk(c)], recv.at[1 - side, chunk(c)], ssem.at[side, c], rsem.at[1 - side, c],
                      axis, beside(axis, side))

    def halo_recv(axis, side, c):
        send, recv, ssem, rsem = (xs, xr, xs_sem, xr_sem) if axis == "sx" else (ys, yr, ys_sem, yr_sem)
        return remote(send.at[side, chunk(c)], recv.at[side, chunk(c)], ssem.at[side, c], rsem.at[side, c],
                      axis, beside(axis, side))

    def detour(side, c):
        q = jnp.where(c >= NC // 2, XW - 1, 0)
        at_seam = (sx == XW - 1) if side == 1 else (sx == XW)
        via = XW + q if side == 1 else XW - 1 - q
        return at_seam & (q != 0), via, lax.rem(c, NC // 2)

    def to_relay(side, c):
        _, via, m = detour(side, c)
        return remote(xs.at[side, chunk(c)], rly.at[m], xs_sem.at[side, c], ry_sem.at[m], "sx", via)

    def relay(c):
        q = jnp.where(c >= NC // 2, XW - 1, 0)
        m = lax.rem(c, NC // 2)
        for side in (0, 1):
            mine = ((sx == XW + q) if side == 1 else (sx == XW - 1 - q)) & (q != 0)

            @pl.when(mine & (c < NC))
            def _():
                dest = XW if side == 1 else XW - 1
                cp = remote(rly.at[m], xr.at[1 - side, chunk(c)], rf_sem.at[m], xr_sem.at[1 - side, c], "sx", dest)
                remote(rly.at[m], rly.at[m], rf_sem.at[m], ry_sem.at[m], "sx", dest).wait_recv()
                cp.start()

    def relay_done(c):
        q = jnp.where(c >= NC // 2, XW - 1, 0)
        m = lax.rem(c, NC // 2)
        for side in (0, 1):
            mine = ((sx == XW + q) if side == 1 else (sx == XW - 1 - q)) & (q != 0)

            @pl.when(mine)
            def _():
                dest = XW if side == 1 else XW - 1
                remote(rly.at[m], xr.at[1 - side, chunk(c)], rf_sem.at[m], xr_sem.at[1 - side, c], "sx", dest).wait_send()

    def par_copy(c):
        return pltpu.make_async_remote_copy(
            snap.at[chunk(c)], peer.at[chunk(c)], ps_sem.at[c], pr_sem.at[c],
            device_id={"par": 1 - par}, device_id_type=MESH,
        )

    col = lax.rem(sx, XW)
    outer = (col == 0) | (col == XW - 1)
    pair = jnp.where(lax.rem(sx, 2) == 0, sx + 1, sx - 1)

    def detours(c):
        i = (c - (NC - 6)) // 2
        return (c >= NC - 6) & (lax.rem(c, 2) == 0) & (i < DETOUR), i

    def par_start(c):
        takes, i = detours(c)
        takes = takes & outer

        @pl.when(takes)
        def _():
            pltpu.make_async_remote_copy(
                snap.at[chunk(c)], rlp.at[i], ps_sem.at[c], dr_sem.at[i],
                device_id={"sx": pair, "par": 1 - par}, device_id_type=MESH,
            ).start()

        @pl.when(jnp.logical_not(takes))
        def _():
            par_copy(c).start()

    def pass_copy(c, i):
        return remote(rlp.at[i], peer.at[chunk(c)], ds_sem.at[i], pr_sem.at[c], "sx", pair)

    def par_pass(c):
        due, i = detours(c)

        @pl.when(due & jnp.logical_not(outer))
        def _():
            remote(rlp.at[i], rlp.at[i], ds_sem.at[i], dr_sem.at[i], "sx", pair).wait_recv()
            pass_copy(c, i).start()

    @pl.loop(0, NC)
    def _(c):
        for cp in load(c):
            cp.start()

    psi_load = pltpu.make_async_copy(psi_hbm, psi, aux_sem.at[0])
    omega_load = pltpu.make_async_copy(omega_hbm, omega_ref, aux_sem.at[1])
    psi_load.start()
    omega_load.start()

    barrier = pltpu.get_barrier_semaphore()
    for d in range(1, nsx):
        pl.semaphore_signal(barrier, inc=1, device_id={"sx": lax.rem(sx + d, nsx)}, device_id_type=MESH)
    for d in range(1, nsy):
        pl.semaphore_signal(barrier, inc=1, device_id={"sy": lax.rem(sy + d, nsy)}, device_id_type=MESH)
    pl.semaphore_signal(barrier, inc=1, device_id={"par": 1 - par}, device_id_type=MESH)
    pl.semaphore_signal(barrier, inc=1, device_id={"sx": pair, "par": 1 - par}, device_id_type=MESH)

    for side in (0, 1):
        @pl.when(jnp.logical_not(has["sx", side]))
        def _():
            @pl.loop(0, S)
            def _(s):
                xr[side, s] = jnp.zeros(xr.shape[2:], BF16)

        @pl.when(jnp.logical_not(has["sy", side]))
        def _():
            @pl.loop(0, S)
            def _(s):
                yr[side, s] = jnp.zeros(yr.shape[2:], BF16)

    row8 = lax.broadcasted_iota(jnp.int32, (1, 8, Z), 1)
    low4 = row8 < 4
    yrow = lax.broadcasted_iota(jnp.int32, (1, Y + 2 * H, Z), 1)
    lane = lax.broadcasted_iota(jnp.int32, (1, Y + 2 * H, Z), 2)
    cut = ((yrow == H - 1) & (sy == 0)) | ((yrow == H + Y - 1) & (sy == nsy - 1))
    ymask = jnp.where(cut, 0.0, 1.0).astype(F32)

    pl.semaphore_wait(barrier, nsx + nsy)

    def x_edges(c):
        for cp in load(c):
            cp.wait()

        @pl.loop(0, CHUNK)
        def _(j):
            s = c * CHUNK + j
            for side, at in ((0, 0), (1, X - H)):
                xs[side, s, 0:H] = u_in[s, at:at + H].astype(BF16)
                xs[side, s, H:2 * H] = k_in[s, at:at + H].astype(BF16)

        for side in (0, 1):
            turn = detour(side, c)[0]

            @pl.when(has["sx", side] & turn)
            def _():
                to_relay(side, c).start()

            @pl.when(has["sx", side] & jnp.logical_not(turn))
            def _():
                halo("sx", side, c).start()

    @pl.loop(0, AHEAD)
    def _(c):
        x_edges(c)

    def half(s, x0, n, tile):
        rows = slice(8 * tile, 8 * tile + 8)
        if x0 < H:
            v = xr[0, s].astype(F32)
            return v[0:H, rows], v[H:2 * H, rows]
        if x0 >= H + X:
            v = xr[1, s].astype(F32)
            return v[0:H, rows], v[H:2 * H, rows]
        return u_in[s, x0 - H:x0 - H + n, rows], k_in[s, x0 - H:x0 - H + n, rows]

    groups = [(x0, H) for x0 in range(0, XE, H)]

    def y_edges(c):
        for side in (0, 1):
            @pl.when(has["sx", side])
            def _():
                halo_recv("sx", side, c).wait_recv()

        @pl.loop(0, CHUNK)
        def _(j):
            s = c * CHUNK + j
            for x0, n in groups:
                u0, k0 = half(s, x0, n, 0)
                u1, k1 = half(s, x0, n, 1)
                p = jnp.where(low4, k0, pltpu.roll(u0, 4, 1))
                q = jnp.where(low4, pltpu.roll(u1, 4, 1), k1)
                ys[0, s, x0 // 2:x0 // 2 + n // 2] = p.reshape(n // 2, 16, Z).astype(BF16)
                ys[1, s, x0 // 2:x0 // 2 + n // 2] = q.reshape(n // 2, 16, Z).astype(BF16)

        for side in (0, 1):
            @pl.when(has["sy", side])
            def _():
                halo("sy", side, c).start()

    def zshift(v, by):
        return pltpu.roll(v, by % Z, 2)

    def yshift(v, by):
        return pltpu.roll(v, by % v.shape[1], 1)

    def sample(s):
        for x0, n in groups:
            u0, k0 = half(s, x0, n, 0)
            u1, k1 = half(s, x0, n, 1)
            lo = yr[0, s, x0 // 2:x0 // 2 + n // 2].astype(F32).reshape(n, 8, Z)
            hi = yr[1, s, x0 // 2:x0 // 2 + n // 2].astype(F32).reshape(n, 8, Z)
            a, b = pltpu.roll(u0, 4, 1), pltpu.roll(u1, 4, 1)
            ua[x0:x0 + n, 0:8] = jnp.where(low4, lo, a)
            ua[x0:x0 + n, 8:16] = jnp.where(low4, a, b)
            ua[x0:x0 + n, 16:24] = jnp.where(low4, b, hi)
            a, b = pltpu.roll(k0, 4, 1), pltpu.roll(k1, 4, 1)
            kk[x0:x0 + n, 0:8] = jnp.where(low4, pltpu.roll(lo, 4, 1), a) * 0.08
            kk[x0:x0 + n, 8:16] = jnp.where(low4, a, b) * 0.08
            kk[x0:x0 + n, 16:24] = jnp.where(low4, b, pltpu.roll(hi, 4, 1)) * 0.08

        cx[0:1] = kk[0:1] + kk[1:2]

        def faces(i, _):
            x = pl.ds(1 + 2 * i, 2)
            k = kk[x]
            fx = k + kk[pl.ds(2 + 2 * i, 2)]
            bx = k + kk[pl.ds(2 * i, 2)]
            fy = k + yshift(k, -1)
            by = yshift(fy, 1)
            fz = k + jnp.where(lane < Z - 1, zshift(k, -1), 0.0)
            bz = k + jnp.where(lane > 0, zshift(k, 1), 0.0)
            dd[x] = 1.0 - (((fx + bx) + (fy + by)) + (fz + bz))
            cx[x] = fx
            cy[x] = fy * ymask
            cz[x] = jnp.where(lane < Z - 1, fz, 0.0)
            return 0

        lax.fori_loop(0, (XE - 2) // 2, faces, 0, unroll=True)

        @pl.when(sx == 0)
        def _():
            cx[H - 1:H] = jnp.zeros((1, Y + 2 * H, Z), F32)

        @pl.when(sx == nsx - 1)
        def _():
            cx[H + X - 1:H + X] = jnp.zeros((1, Y + 2 * H, Z), F32)

        def stencil(src, x0):
            x = pl.ds(x0, 2)
            u = src[x]
            y_c, z_c = cy[x], cz[x]
            out = dd[x] * u
            out += cx[x] * src[pl.ds(x0 + 1, 2)] + cx[pl.ds(x0 - 1, 2)] * src[pl.ds(x0 - 1, 2)]
            out += y_c * yshift(u, -1) + yshift(y_c * u, 1)
            out += z_c * zshift(u, -1) + zshift(z_c * u, 1)
            return out

        src, dst = ua, ub
        for step in range(STEPS - 1):
            first = 1 + step

            def advance(i, _, src=src, dst=dst, first=first):
                dst[pl.ds(first + 2 * i, 2)] = stencil(src, first + 2 * i)
                return 0

            lax.fori_loop(0, (XE - 2 * first) // 2, advance, 0, unroll=True)
            src, dst = dst, src

        def last(i, _, src=src):
            v = stencil(src, H + 2 * i)
            v0, v1, v2 = (pltpu.roll(v[:, 8 * t:8 * t + 8], 4, 1) for t in range(3))
            a, b = jnp.where(low4, v0, v1), jnp.where(low4, v1, v2)
            o = jnp.concatenate([a, b], axis=1)
            u_in[s, pl.ds(2 * i, 2)] = o
            snap[s, pl.ds(2 * i, 2)] = o.astype(BF16)
            return 0

        lax.fori_loop(0, X // 2, last, 0, unroll=True)

    y_edges(0)
    relay(jnp.int32(1))
    relay(jnp.int32(2))
    y_edges(1)

    SB, RB = 16, 16

    def corange(sb):
        @pl.loop(0, R // RB)
        def _(rb):
            val = None
            for x in range(0, X, 2):
                left = jnp.concatenate([psi[pl.ds(rb * RB, RB), x + d].reshape(RB * Y, Z) for d in range(2)], axis=1)
                right = jnp.concatenate([snap[pl.ds(sb * SB, SB), x + d].reshape(SB * Y, Z) for d in range(2)], axis=1)
                term = lax.dot_general(left, right, (((1,), (1,)), ((), ())), preferred_element_type=F32)
                val = term if val is None else val + term
            w_r = lax.rem(lax.broadcasted_iota(jnp.int32, (RB * Y, SB * Y), 0), Y)
            w_c = lax.rem(lax.broadcasted_iota(jnp.int32, (RB * Y, SB * Y), 1), Y)
            val = jnp.where(w_r == w_c, val, 0.0).reshape(RB, Y, SB * Y)
            red[sb, pl.ds(rb * RB, RB)] = jnp.sum(val, axis=1)

    psi_load.wait()

    @pl.loop(0, NC)
    def _(c):
        for sb in range(S // SB - 1):
            @pl.when(c == (sb + 1) * SB // CHUNK)
            def _():
                corange(sb)

        @pl.when(c + AHEAD < NC)
        def _():
            x_edges(c + AHEAD)

        upto = jnp.minimum(2 * c + 4, c + 8)

        @pl.loop(jnp.minimum(2 * c + 2, c + 8 - 1) + 1, upto + 1)
        def _(i):
            relay(i)

        @pl.when(c + 2 < NC)
        def _():
            y_edges(c + 2)

        for side in (0, 1):
            @pl.when(has["sy", side])
            def _():
                halo_recv("sy", side, c).wait_recv()

        @pl.loop(0, CHUNK)
        def _(j):
            sample(c * CHUNK + j)

        @pl.when(c < NC - HELD)
        def _():
            par_start(c)

        par_pass(c - LAG)

    corange(S // SB - 1)

    g_r = lax.broadcasted_iota(jnp.int32, (SB, SB * Y), 0)
    g_c = lax.broadcasted_iota(jnp.int32, (SB, SB * Y), 1) // Y
    group = jnp.where(g_r == g_c, 1.0, 0.0).astype(F32)
    part[...] = jnp.concatenate([
        lax.dot_general(group, red[q], (((1,), (1,)), ((), ())), preferred_element_type=F32, precision=lax.Precision.HIGHEST)
        for q in range(S // SB)], axis=1)

    def gather(axis, d, src, dst, ssem, rsem):
        n = dst.shape[0]
        return remote(src, dst.at[pos[axis]], ssem.at[d], rsem.at[d], axis, lax.rem(pos[axis] + d, n))

    def gather_recv(axis, d, src, dst, ssem, rsem):
        n = dst.shape[0]
        return remote(src, dst.at[lax.rem(pos[axis] + n - d, n)], ssem.at[d], rsem.at[d], axis, lax.rem(pos[axis] + d, n))

    for d in range(1, nsx):
        gather("sx", d, part, gat1, a1s_sem, a1r_sem).start()

    @pl.loop(NC - HELD, NC)
    def _(c):
        par_start(c)

    @pl.loop(NC - LAG, NC)
    def _(c):
        par_pass(c)

    omega_load.wait()
    i_r = lax.broadcasted_iota(jnp.int32, (RD * Y, R), 0) // Y
    i_j = lax.broadcasted_iota(jnp.int32, (RD * Y, R), 1)
    pick = jnp.where(i_j == i_r + par * RD, 1.0, 0.0).astype(BF16)
    cols = lax.dot_general(pick, omega_ref[...], (((1,), (1,)), ((), ())), preferred_element_type=F32).astype(BF16)
    total = omega_ref.shape[0]
    WB = 256

    @pl.loop(0, total * Y // WB)
    def _(b):
        e_s = lax.broadcasted_iota(jnp.int32, (total, WB), 0)
        e_c = lax.broadcasted_iota(jnp.int32, (total, WB), 1) + b * WB
        spread = jnp.where(e_s == lax.rem(e_c // Y + par * S, total), 1.0, 0.0).astype(BF16)
        wide = jnp.dot(cols, spread, preferred_element_type=F32)
        w_r = lax.rem(lax.broadcasted_iota(jnp.int32, (RD * Y, WB), 0), Y)
        w_c = lax.rem(lax.broadcasted_iota(jnp.int32, (RD * Y, WB), 1), Y)
        w_ref[:, pl.ds(pl.multiple_of(b * WB, WB), WB)] = jnp.where(w_r == w_c, wide, 0.0).astype(BF16)


    def range_part(x0, weights, source, lo, n):
        right = jnp.concatenate([source[lo:lo + n, x0 + d].reshape(n * Y, Z) for d in range(2)], axis=1)
        return jnp.dot(weights, right, preferred_element_type=F32)

    for x0 in range(0, X, 2):
        t = range_part(x0, w_ref[:, 0:S * Y], snap, 0, S)
        for d in range(2):
            acc[x0 + d] = t[:, d * Z:(d + 1) * Z]

    gat1[pl.ds(sx, 1)] = part[...][None]
    for d in range(1, nsx):
        gather("sx", d, part, gat1, a1s_sem, a1r_sem).wait_send()
        gather_recv("sx", d, part, gat1, a1s_sem, a1r_sem).wait_recv()
    tot = gat1[0]
    for i in range(1, nsx):
        tot += gat1[i]
    part2[...] = tot
    for d in range(1, nsy):
        gather("sy", d, part2, gat2, a2s_sem, a2r_sem).start()

    HALF = S // 2
    for c in range(NC // 2):
        par_copy(c).wait_recv()
    for x0 in range(0, X, 2):
        t = range_part(x0, w_ref[:, S * Y:(S + HALF) * Y], peer, 0, HALF)
        for d in range(2):
            acc[x0 + d] = acc[x0 + d] + t[:, d * Z:(d + 1) * Z]

    gat2[pl.ds(sy, 1)] = part2[...][None]
    for d in range(1, nsy):
        gather("sy", d, part2, gat2, a2s_sem, a2r_sem).wait_send()
        gather_recv("sy", d, part2, gat2, a2s_sem, a2r_sem).wait_recv()
    tot = gat2[0]
    for i in range(1, nsy):
        tot += gat2[i]
    for q in range(S // SB):
        cor_ref[q * SB:(q + 1) * SB] = tot[:, q * R:(q + 1) * R]

    for c in range(NC // 2, NC):
        par_copy(c).wait_recv()

    for x0 in range(0, X, 2):
        t = range_part(x0, w_ref[:, (S + HALF) * Y:2 * S * Y], peer, HALF, HALF)
        for d in range(2):
            acc[x0 + d] = acc[x0 + d] + t[:, d * Z:(d + 1) * Z]

    @pl.loop(0, NC)
    def _(c):
        for side in (0, 1):
            for axis in ("sx", "sy"):
                @pl.when(has[axis, side])
                def _():
                    halo(axis, side, c).wait_send()
        relay_done(c)
        due, i = detours(c)

        @pl.when(due & jnp.logical_not(outer))
        def _():
            pass_copy(c, i).wait_send()

        par_copy(c).wait_send()


def store(fin_ref, acc_ref, cor_ref, prev, cprev_ref, fin_hbm, rng_hbm, cor_out, rng, sem):
    RD, X, Y, Z = prev.shape
    N = PIECES
    n, m = RD // N, fin_ref.shape[0] // N
    fins = [pltpu.make_async_copy(fin_ref.at[pl.ds(p * m, m)], fin_hbm.at[pl.ds(p * m, m)], sem.at[0, p]) for p in range(N)]
    outs = [pltpu.make_async_copy(rng.at[pl.ds(p * n, n)], rng_hbm.at[pl.ds(p * n, n)], sem.at[1, p]) for p in range(N)]
    for cp in fins:
        cp.start()
    cor_out[...] = cprev_ref[...] + cor_ref[...]
    for p in range(N):
        def add(x, _, p=p):
            new = acc_ref[x, p * n * Y:(p + 1) * n * Y].reshape(n, Y, Z)
            rng[p * n:(p + 1) * n, x] = (prev[p * n:(p + 1) * n, x].astype(F32) + new).astype(BF16)
            return 0

        lax.fori_loop(0, X, add, 0, unroll=True)
        outs[p].start()
    for cp in fins + outs:
        cp.wait()


def per_device(sizes, initial_state, conductivity, omega, psi, range_prev, corange_prev):
    S, X, Y, Z = initial_state.shape
    R, RD = psi.shape[0], range_prev.shape[0]
    nsx, nsy = sizes
    NC = S // CHUNK
    E = (X + 2 * H, Y + 2 * H, Z)
    dma = pltpu.SemaphoreType.DMA
    scratch = [
        pltpu.VMEM((S, X, Y, Z), F32),
        pltpu.VMEM((2, S, 2 * H, Y, Z), BF16),
        pltpu.VMEM((2, S, 2 * H, Y, Z), BF16),
        pltpu.VMEM((NC // 2, CHUNK, 2 * H, Y, Z), BF16),
        pltpu.VMEM((DETOUR, CHUNK, X, Y, Z), BF16),
        pltpu.VMEM((2, S, E[0] // 2, 16, Z), BF16),
        pltpu.VMEM((2, S, E[0] // 2, 16, Z), BF16),
        pltpu.VMEM((S, X, Y, Z), BF16),
        pltpu.VMEM((S, X, Y, Z), BF16),
        pltpu.VMEM((R, X, Y, Z), BF16),
        pltpu.VMEM(omega.shape, BF16),
        pltpu.VMEM((RD * Y, 2 * S * Y), BF16),
        pltpu.VMEM((S // 16, R, 16 * Y), F32),
        pltpu.VMEM((R * S // Z, Z), F32),
        pltpu.VMEM((nsx, R * S // Z, Z), F32),
        pltpu.VMEM((R * S // Z, Z), F32),
        pltpu.VMEM((nsy, R * S // Z, Z), F32),
    ] + [pltpu.VMEM(E, F32)] * 7 + [
        dma((2, NC)), dma((2,)), dma((2, NC)), dma((2, NC)), dma((NC // 2,)), dma((NC // 2,)),
        dma((2, NC)), dma((2, NC)), dma((NC,)), dma((NC,)), dma((DETOUR,)), dma((DETOUR,)),
        dma((nsx,)), dma((nsx,)), dma((nsy,)), dma((nsy,)),
    ]
    any_ = pl.BlockSpec(memory_space=pl.ANY)
    hbm = pl.BlockSpec(memory_space=pltpu.HBM)
    vmem = pl.BlockSpec(memory_space=pltpu.VMEM)
    final, sketch, corange = pl.pallas_call(
        kernel,
        out_shape=(
            jax.ShapeDtypeStruct(initial_state.shape, F32),
            jax.ShapeDtypeStruct((X, RD * Y, Z), F32),
            jax.ShapeDtypeStruct(corange_prev.shape[::-1], F32),
        ),
        in_specs=[hbm, hbm, hbm, hbm],
        out_specs=(vmem, vmem, vmem),
        scratch_shapes=scratch,
        compiler_params=pltpu.CompilerParams(
            collective_id=0, has_side_effects=True, vmem_limit_bytes=VMEM_MIB * 2**20
        ),
    )(initial_state, conductivity, pltpu.with_memory_space_constraint(omega, pltpu.HBM), psi)
    final, sketch, corange = pl.pallas_call(
        store,
        out_shape=(
            jax.ShapeDtypeStruct(initial_state.shape, F32),
            jax.ShapeDtypeStruct(range_prev.shape, BF16),
            jax.ShapeDtypeStruct(corange_prev.shape[::-1], F32),
        ),
        in_specs=[vmem, vmem, vmem, vmem, vmem],
        out_specs=(any_, any_, vmem),
        scratch_shapes=[pltpu.VMEM(range_prev.shape, BF16), dma((2, PIECES))],
        compiler_params=pltpu.CompilerParams(vmem_limit_bytes=16 * 2**20),
    )(final, sketch, corange, range_prev, corange_prev.T)
    return final, sketch, corange.T


def solution(mesh):
    in_specs = (
        P("par", "sx", "sy", None),
        P("par", "sx", "sy", None),
        P(),
        P(None, "sx", "sy", None),
        P("par", "sx", "sy", None),
        P(None, "par"),
    )
    out_specs = (P("par", "sx", "sy", None), P("par", "sx", "sy", None), P(None, "par"))
    sizes = (mesh.shape["sx"], mesh.shape["sy"])
    return jax.shard_map(
        functools.partial(per_device, sizes), mesh=mesh, in_specs=in_specs, out_specs=out_specs, check_vma=False
    )
```

```python
import functools

import jax
import jax.numpy as jnp
from jax import lax
from jax.experimental import pallas as pl
from jax.experimental.pallas import tpu as pltpu
from jax.sharding import PartitionSpec as P

STEPS = 4
H = STEPS
MESH = pl.DeviceIdType.MESH
F32 = jnp.float32
BF16 = jnp.bfloat16
CHUNK = 2
AHEAD = 16
HELD = 4
VMEM_MIB = 44
PIECES = 2
DETOUR = 1
LAG = 3


def kernel(
    u_hbm, k_hbm, omega_hbm, psi_hbm,
    u_in, acc, cor_ref,
    k_in, xs, xr, rly, rlp, ys, yr, snap, peer, psi, omega_ref, w_ref, red, part, gat1, part2, gat2,
    ua, ub, kk, cx, cy, cz, dd,
    load_sem, aux_sem, xs_sem, xr_sem, ry_sem, rf_sem, ys_sem, yr_sem, ps_sem, pr_sem, ds_sem, dr_sem,
    a1s_sem, a1r_sem, a2s_sem, a2r_sem,
):
    S, X, Y, Z = u_in.shape
    NC = S // CHUNK
    XE = X + 2 * H
    R = psi.shape[0]
    RD = acc.shape[1] // Y
    sx, sy, par = lax.axis_index("sx"), lax.axis_index("sy"), lax.axis_index("par")
    nsx, nsy = gat1.shape[0], gat2.shape[0]
    has = {("sx", 0): sx > 0, ("sx", 1): sx < nsx - 1, ("sy", 0): sy > 0, ("sy", 1): sy < nsy - 1}
    pos = {"sx": sx, "sy": sy}

    def chunk(c):
        return pl.ds(c * CHUNK, CHUNK)

    def load(c):
        return (
            pltpu.make_async_copy(u_hbm.at[chunk(c)], u_in.at[chunk(c)], load_sem.at[0, c]),
            pltpu.make_async_copy(k_hbm.at[chunk(c)], k_in.at[chunk(c)], load_sem.at[1, c]),
        )

    XW = nsx // 2

    def remote(src, dst, ssem, rsem, axis, other):
        return pltpu.make_async_remote_copy(src, dst, ssem, rsem, device_id={axis: other}, device_id_type=MESH)

    def beside(axis, side):
        n = nsx if axis == "sx" else nsy
        return jnp.maximum(pos[axis] - 1, 0) if side == 0 else jnp.minimum(pos[axis] + 1, n - 1)

    def halo(axis, side, c):
        send, recv, ssem, rsem = (xs, xr, xs_sem, xr_sem) if axis == "sx" else (ys, yr, ys_sem, yr_sem)
        return remote(send.at[side, chunk(c)], recv.at[1 - side, chunk(c)], ssem.at[side, c], rsem.at[1 - side, c],
                      axis, beside(axis, side))

    def halo_recv(axis, side, c):
        send, recv, ssem, rsem = (xs, xr, xs_sem, xr_sem) if axis == "sx" else (ys, yr, ys_sem, yr_sem)
        return remote(send.at[side, chunk(c)], recv.at[side, chunk(c)], ssem.at[side, c], rsem.at[side, c],
                      axis, beside(axis, side))

    def detour(side, c):
        q = jnp.where(c >= NC // 2, XW - 1, 0)
        at_seam = (sx == XW - 1) if side == 1 else (sx == XW)
        via = XW + q if side == 1 else XW - 1 - q
        return at_seam & (q != 0), via, lax.rem(c, NC // 2)

    def to_relay(side, c):
        _, via, m = detour(side, c)
        return remote(xs.at[side, chunk(c)], rly.at[m], xs_sem.at[side, c], ry_sem.at[m], "sx", via)

    def relay(c):
        q = jnp.where(c >= NC // 2, XW - 1, 0)
        m = lax.rem(c, NC // 2)
        for side in (0, 1):
            mine = ((sx == XW + q) if side == 1 else (sx == XW - 1 - q)) & (q != 0)

            @pl.when(mine & (c < NC))
            def _():
                dest = XW if side == 1 else XW - 1
                cp = remote(rly.at[m], xr.at[1 - side, chunk(c)], rf_sem.at[m], xr_sem.at[1 - side, c], "sx", dest)
                remote(rly.at[m], rly.at[m], rf_sem.at[m], ry_sem.at[m], "sx", dest).wait_recv()
                cp.start()

    def relay_done(c):
        q = jnp.where(c >= NC // 2, XW - 1, 0)
        m = lax.rem(c, NC // 2)
        for side in (0, 1):
            mine = ((sx == XW + q) if side == 1 else (sx == XW - 1 - q)) & (q != 0)

            @pl.when(mine)
            def _():
                dest = XW if side == 1 else XW - 1
                remote(rly.at[m], xr.at[1 - side, chunk(c)], rf_sem.at[m], xr_sem.at[1 - side, c], "sx", dest).wait_send()

    def par_copy(c):
        return pltpu.make_async_remote_copy(
            snap.at[chunk(c)], peer.at[chunk(c)], ps_sem.at[c], pr_sem.at[c],
            device_id={"par": 1 - par}, device_id_type=MESH,
        )

    col = lax.rem(sx, XW)
    outer = (col == 0) | (col == XW - 1)
    pair = jnp.where(lax.rem(sx, 2) == 0, sx + 1, sx - 1)

    def detours(c):
        i = (c - (NC - 6)) // 2
        return (c >= NC - 6) & (lax.rem(c, 2) == 0) & (i < DETOUR), i

    def par_start(c):
        takes, i = detours(c)
        takes = takes & outer

        @pl.when(takes)
        def _():
            pltpu.make_async_remote_copy(
                snap.at[chunk(c)], rlp.at[i], ps_sem.at[c], dr_sem.at[i],
                device_id={"sx": pair, "par": 1 - par}, device_id_type=MESH,
            ).start()

        @pl.when(jnp.logical_not(takes))
        def _():
            par_copy(c).start()

    def pass_copy(c, i):
        return remote(rlp.at[i], peer.at[chunk(c)], ds_sem.at[i], pr_sem.at[c], "sx", pair)

    def par_pass(c):
        due, i = detours(c)

        @pl.when(due & jnp.logical_not(outer))
        def _():
            remote(rlp.at[i], rlp.at[i], ds_sem.at[i], dr_sem.at[i], "sx", pair).wait_recv()
            pass_copy(c, i).start()

    @pl.loop(0, NC)
    def _(c):
        for cp in load(c):
            cp.start()

    psi_load = pltpu.make_async_copy(psi_hbm, psi, aux_sem.at[0])
    omega_load = pltpu.make_async_copy(omega_hbm, omega_ref, aux_sem.at[1])
    psi_load.start()
    omega_load.start()

    barrier = pltpu.get_barrier_semaphore()
    for d in range(1, nsx):
        pl.semaphore_signal(barrier, inc=1, device_id={"sx": lax.rem(sx + d, nsx)}, device_id_type=MESH)
    for d in range(1, nsy):
        pl.semaphore_signal(barrier, inc=1, device_id={"sy": lax.rem(sy + d, nsy)}, device_id_type=MESH)
    pl.semaphore_signal(barrier, inc=1, device_id={"par": 1 - par}, device_id_type=MESH)
    pl.semaphore_signal(barrier, inc=1, device_id={"sx": pair, "par": 1 - par}, device_id_type=MESH)

    for side in (0, 1):
        @pl.when(jnp.logical_not(has["sx", side]))
        def _():
            @pl.loop(0, S)
            def _(s):
                xr[side, s] = jnp.zeros(xr.shape[2:], BF16)

        @pl.when(jnp.logical_not(has["sy", side]))
        def _():
            @pl.loop(0, S)
            def _(s):
                yr[side, s] = jnp.zeros(yr.shape[2:], BF16)

    row8 = lax.broadcasted_iota(jnp.int32, (1, 8, Z), 1)
    low4 = row8 < 4
    yrow = lax.broadcasted_iota(jnp.int32, (1, Y + 2 * H, Z), 1)
    lane = lax.broadcasted_iota(jnp.int32, (1, Y + 2 * H, Z), 2)
    cut = ((yrow == H - 1) & (sy == 0)) | ((yrow == H + Y - 1) & (sy == nsy - 1))
    ymask = jnp.where(cut, 0.0, 1.0).astype(F32)

    pl.semaphore_wait(barrier, nsx + nsy)

    def x_edges(c):
        for cp in load(c):
            cp.wait()

        @pl.loop(0, CHUNK)
        def _(j):
            s = c * CHUNK + j
            for side, at in ((0, 0), (1, X - H)):
                xs[side, s, 0:H] = u_in[s, at:at + H].astype(BF16)
                xs[side, s, H:2 * H] = k_in[s, at:at + H].astype(BF16)

        for side in (0, 1):
            turn = detour(side, c)[0]

            @pl.when(has["sx", side] & turn)
            def _():
                to_relay(side, c).start()

            @pl.when(has["sx", side] & jnp.logical_not(turn))
            def _():
                halo("sx", side, c).start()

    @pl.loop(0, AHEAD)
    def _(c):
        x_edges(c)

    def half(s, x0, n, tile):
        rows = slice(8 * tile, 8 * tile + 8)
        if x0 < H:
            v = xr[0, s].astype(F32)
            return v[0:H, rows], v[H:2 * H, rows]
        if x0 >= H + X:
            v = xr[1, s].astype(F32)
            return v[0:H, rows], v[H:2 * H, rows]
        return u_in[s, x0 - H:x0 - H + n, rows], k_in[s, x0 - H:x0 - H + n, rows]

    groups = [(x0, H) for x0 in range(0, XE, H)]

    def y_edges(c):
        for side in (0, 1):
            @pl.when(has["sx", side])
            def _():
                halo_recv("sx", side, c).wait_recv()

        @pl.loop(0, CHUNK)
        def _(j):
            s = c * CHUNK + j
            for x0, n in groups:
                u0, k0 = half(s, x0, n, 0)
                u1, k1 = half(s, x0, n, 1)
                p = jnp.where(low4, k0, pltpu.roll(u0, 4, 1))
                q = jnp.where(low4, pltpu.roll(u1, 4, 1), k1)
                ys[0, s, x0 // 2:x0 // 2 + n // 2] = p.reshape(n // 2, 16, Z).astype(BF16)
                ys[1, s, x0 // 2:x0 // 2 + n // 2] = q.reshape(n // 2, 16, Z).astype(BF16)

        for side in (0, 1):
            @pl.when(has["sy", side])
            def _():
                halo("sy", side, c).start()

    def zshift(v, by):
        return pltpu.roll(v, by % Z, 2)

    def yshift(v, by):
        return pltpu.roll(v, by % v.shape[1], 1)

    def sample(s):
        for x0, n in groups:
            u0, k0 = half(s, x0, n, 0)
            u1, k1 = half(s, x0, n, 1)
            lo = yr[0, s, x0 // 2:x0 // 2 + n // 2].astype(F32).reshape(n, 8, Z)
            hi = yr[1, s, x0 // 2:x0 // 2 + n // 2].astype(F32).reshape(n, 8, Z)
            a, b = pltpu.roll(u0, 4, 1), pltpu.roll(u1, 4, 1)
            ua[x0:x0 + n, 0:8] = jnp.where(low4, lo, a)
            ua[x0:x0 + n, 8:16] = jnp.where(low4, a, b)
            ua[x0:x0 + n, 16:24] = jnp.where(low4, b, hi)
            a, b = pltpu.roll(k0, 4, 1), pltpu.roll(k1, 4, 1)
            kk[x0:x0 + n, 0:8] = jnp.where(low4, pltpu.roll(lo, 4, 1), a) * 0.08
            kk[x0:x0 + n, 8:16] = jnp.where(low4, a, b) * 0.08
            kk[x0:x0 + n, 16:24] = jnp.where(low4, b, pltpu.roll(hi, 4, 1)) * 0.08

        cx[0:1] = kk[0:1] + kk[1:2]

        def faces(i, _):
            x = pl.ds(1 + 2 * i, 2)
            k = kk[x]
            fx = k + kk[pl.ds(2 + 2 * i, 2)]
            bx = k + kk[pl.ds(2 * i, 2)]
            fy = k + yshift(k, -1)
            by = yshift(fy, 1)
            fz = k + jnp.where(lane < Z - 1, zshift(k, -1), 0.0)
            bz = k + jnp.where(lane > 0, zshift(k, 1), 0.0)
            dd[x] = 1.0 - (((fx + bx) + (fy + by)) + (fz + bz))
            cx[x] = fx
            cy[x] = fy * ymask
            cz[x] = jnp.where(lane < Z - 1, fz, 0.0)
            return 0

        lax.fori_loop(0, (XE - 2) // 2, faces, 0, unroll=True)

        @pl.when(sx == 0)
        def _():
            cx[H - 1:H] = jnp.zeros((1, Y + 2 * H, Z), F32)

        @pl.when(sx == nsx - 1)
        def _():
            cx[H + X - 1:H + X] = jnp.zeros((1, Y + 2 * H, Z), F32)

        def stencil(src, x0):
            x = pl.ds(x0, 2)
            u = src[x]
            y_c, z_c = cy[x], cz[x]
            out = dd[x] * u
            out += cx[x] * src[pl.ds(x0 + 1, 2)] + cx[pl.ds(x0 - 1, 2)] * src[pl.ds(x0 - 1, 2)]
            out += y_c * yshift(u, -1) + yshift(y_c * u, 1)
            out += z_c * zshift(u, -1) + zshift(z_c * u, 1)
            return out

        src, dst = ua, ub
        for step in range(STEPS - 1):
            first = 1 + step

            def advance(i, _, src=src, dst=dst, first=first):
                dst[pl.ds(first + 2 * i, 2)] = stencil(src, first + 2 * i)
                return 0

            lax.fori_loop(0, (XE - 2 * first) // 2, advance, 0, unroll=True)
            src, dst = dst, src

        def last(i, _, src=src):
            v = stencil(src, H + 2 * i)
            v0, v1, v2 = (pltpu.roll(v[:, 8 * t:8 * t + 8], 4, 1) for t in range(3))
            a, b = jnp.where(low4, v0, v1), jnp.where(low4, v1, v2)
            o = jnp.concatenate([a, b], axis=1)
            u_in[s, pl.ds(2 * i, 2)] = o
            snap[s, pl.ds(2 * i, 2)] = o.astype(BF16)
            return 0

        lax.fori_loop(0, X // 2, last, 0, unroll=True)

    y_edges(0)
    relay(jnp.int32(1))
    relay(jnp.int32(2))
    y_edges(1)

    SB, RB = 16, 16

    def corange(sb):
        @pl.loop(0, R // RB)
        def _(rb):
            val = None
            for x in range(0, X, 2):
                left = jnp.concatenate([psi[pl.ds(rb * RB, RB), x + d].reshape(RB * Y, Z) for d in range(2)], axis=1)
                right = jnp.concatenate([snap[pl.ds(sb * SB, SB), x + d].reshape(SB * Y, Z) for d in range(2)], axis=1)
                term = lax.dot_general(left, right, (((1,), (1,)), ((), ())), preferred_element_type=F32)
                val = term if val is None else val + term
            w_r = lax.rem(lax.broadcasted_iota(jnp.int32, (RB * Y, SB * Y), 0), Y)
            w_c = lax.rem(lax.broadcasted_iota(jnp.int32, (RB * Y, SB * Y), 1), Y)
            val = jnp.where(w_r == w_c, val, 0.0).reshape(RB, Y, SB * Y)
            red[sb, pl.ds(rb * RB, RB)] = jnp.sum(val, axis=1)

    psi_load.wait()

    @pl.loop(0, NC)
    def _(c):
        for sb in range(S // SB - 1):
            @pl.when(c == (sb + 1) * SB // CHUNK)
            def _():
                corange(sb)

        @pl.when(c + AHEAD < NC)
        def _():
            x_edges(c + AHEAD)

        upto = jnp.minimum(2 * c + 4, c + 8)

        @pl.loop(jnp.minimum(2 * c + 2, c + 8 - 1) + 1, upto + 1)
        def _(i):
            relay(i)

        @pl.when(c + 2 < NC)
        def _():
            y_edges(c + 2)

        for side in (0, 1):
            @pl.when(has["sy", side])
            def _():
                halo_recv("sy", side, c).wait_recv()

        @pl.loop(0, CHUNK)
        def _(j):
            sample(c * CHUNK + j)

        @pl.when(c < NC - HELD)
        def _():
            par_start(c)

        par_pass(c - LAG)

    corange(S // SB - 1)

    g_r = lax.broadcasted_iota(jnp.int32, (SB, SB * Y), 0)
    g_c = lax.broadcasted_iota(jnp.int32, (SB, SB * Y), 1) // Y
    group = jnp.where(g_r == g_c, 1.0, 0.0).astype(F32)
    part[...] = jnp.concatenate([
        lax.dot_general(group, red[q], (((1,), (1,)), ((), ())), preferred_element_type=F32, precision=lax.Precision.HIGHEST)
        for q in range(S // SB)], axis=1)

    def gather(axis, d, src, dst, ssem, rsem):
        n = dst.shape[0]
        return remote(src, dst.at[pos[axis]], ssem.at[d], rsem.at[d], axis, lax.rem(pos[axis] + d, n))

    def gather_recv(axis, d, src, dst, ssem, rsem):
        n = dst.shape[0]
        return remote(src, dst.at[lax.rem(pos[axis] + n - d, n)], ssem.at[d], rsem.at[d], axis, lax.rem(pos[axis] + d, n))

    for d in range(1, nsx):
        gather("sx", d, part, gat1, a1s_sem, a1r_sem).start()

    @pl.loop(NC - HELD, NC)
    def _(c):
        par_start(c)

    @pl.loop(NC - LAG, NC)
    def _(c):
        par_pass(c)

    omega_load.wait()
    i_r = lax.broadcasted_iota(jnp.int32, (RD * Y, R), 0) // Y
    i_j = lax.broadcasted_iota(jnp.int32, (RD * Y, R), 1)
    pick = jnp.where(i_j == i_r + par * RD, 1.0, 0.0).astype(BF16)
    cols = lax.dot_general(pick, omega_ref[...], (((1,), (1,)), ((), ())), preferred_element_type=F32).astype(BF16)
    total = omega_ref.shape[0]
    WB = 256

    @pl.loop(0, total * Y // WB)
    def _(b):
        e_s = lax.broadcasted_iota(jnp.int32, (total, WB), 0)
        e_c = lax.broadcasted_iota(jnp.int32, (total, WB), 1) + b * WB
        spread = jnp.where(e_s == lax.rem(e_c // Y + par * S, total), 1.0, 0.0).astype(BF16)
        wide = jnp.dot(cols, spread, preferred_element_type=F32)
        w_r = lax.rem(lax.broadcasted_iota(jnp.int32, (RD * Y, WB), 0), Y)
        w_c = lax.rem(lax.broadcasted_iota(jnp.int32, (RD * Y, WB), 1), Y)
        w_ref[:, pl.ds(pl.multiple_of(b * WB, WB), WB)] = jnp.where(w_r == w_c, wide, 0.0).astype(BF16)


    def range_part(x0, weights, source, lo, n):
        right = jnp.concatenate([source[lo:lo + n, x0 + d].reshape(n * Y, Z) for d in range(2)], axis=1)
        return jnp.dot(weights, right, preferred_element_type=F32)

    for x0 in range(0, X, 2):
        t = range_part(x0, w_ref[:, 0:S * Y], snap, 0, S)
        for d in range(2):
            acc[x0 + d] = t[:, d * Z:(d + 1) * Z]

    gat1[pl.ds(sx, 1)] = part[...][None]
    for d in range(1, nsx):
        gather("sx", d, part, gat1, a1s_sem, a1r_sem).wait_send()
        gather_recv("sx", d, part, gat1, a1s_sem, a1r_sem).wait_recv()
    tot = gat1[0]
    for i in range(1, nsx):
        tot += gat1[i]
    part2[...] = tot
    for d in range(1, nsy):
        gather("sy", d, part2, gat2, a2s_sem, a2r_sem).start()

    HALF = S // 2
    for c in range(NC // 2):
        par_copy(c).wait_recv()
    for x0 in range(0, X, 2):
        t = range_part(x0, w_ref[:, S * Y:(S + HALF) * Y], peer, 0, HALF)
        for d in range(2):
            acc[x0 + d] = acc[x0 + d] + t[:, d * Z:(d + 1) * Z]

    gat2[pl.ds(sy, 1)] = part2[...][None]
    for d in range(1, nsy):
        gather("sy", d, part2, gat2, a2s_sem, a2r_sem).wait_send()
        gather_recv("sy", d, part2, gat2, a2s_sem, a2r_sem).wait_recv()
    tot = gat2[0]
    for i in range(1, nsy):
        tot += gat2[i]
    for q in range(S // SB):
        cor_ref[q * SB:(q + 1) * SB] = tot[:, q * R:(q + 1) * R]

    for c in range(NC // 2, NC):
        par_copy(c).wait_recv()

    for x0 in range(0, X, 2):
        t = range_part(x0, w_ref[:, (S + HALF) * Y:2 * S * Y], peer, HALF, HALF)
        for d in range(2):
            acc[x0 + d] = acc[x0 + d] + t[:, d * Z:(d + 1) * Z]

    @pl.loop(0, NC)
    def _(c):
        for side in (0, 1):
            for axis in ("sx", "sy"):
                @pl.when(has[axis, side])
                def _():
                    halo(axis, side, c).wait_send()
        relay_done(c)
        due, i = detours(c)

        @pl.when(due & jnp.logical_not(outer))
        def _():
            pass_copy(c, i).wait_send()

        par_copy(c).wait_send()


def store(fin_ref, acc_ref, cor_ref, prev, cprev_ref, fin_hbm, rng_hbm, cor_out, rng, sem):
    RD, X, Y, Z = prev.shape
    N = PIECES
    n, m = RD // N, fin_ref.shape[0] // N
    fins = [pltpu.make_async_copy(fin_ref.at[pl.ds(p * m, m)], fin_hbm.at[pl.ds(p * m, m)], sem.at[0, p]) for p in range(N)]
    outs = [pltpu.make_async_copy(rng.at[pl.ds(p * n, n)], rng_hbm.at[pl.ds(p * n, n)], sem.at[1, p]) for p in range(N)]
    for cp in fins:
        cp.start()
    cor_out[...] = cprev_ref[...] + cor_ref[...]
    for p in range(N):
        def add(x, _, p=p):
            new = acc_ref[x, p * n * Y:(p + 1) * n * Y].reshape(n, Y, Z)
            rng[p * n:(p + 1) * n, x] = (prev[p * n:(p + 1) * n, x].astype(F32) + new).astype(BF16)
            return 0

        lax.fori_loop(0, X, add, 0, unroll=True)
        outs[p].start()
    for cp in fins + outs:
        cp.wait()


def per_device(sizes, initial_state, conductivity, omega, psi, range_prev, corange_prev):
    S, X, Y, Z = initial_state.shape
    R, RD = psi.shape[0], range_prev.shape[0]
    nsx, nsy = sizes
    NC = S // CHUNK
    E = (X + 2 * H, Y + 2 * H, Z)
    dma = pltpu.SemaphoreType.DMA
    scratch = [
        pltpu.VMEM((S, X, Y, Z), F32),
        pltpu.VMEM((2, S, 2 * H, Y, Z), BF16),
        pltpu.VMEM((2, S, 2 * H, Y, Z), BF16),
        pltpu.VMEM((NC // 2, CHUNK, 2 * H, Y, Z), BF16),
        pltpu.VMEM((DETOUR, CHUNK, X, Y, Z), BF16),
        pltpu.VMEM((2, S, E[0] // 2, 16, Z), BF16),
        pltpu.VMEM((2, S, E[0] // 2, 16, Z), BF16),
        pltpu.VMEM((S, X, Y, Z), BF16),
        pltpu.VMEM((S, X, Y, Z), BF16),
        pltpu.VMEM((R, X, Y, Z), BF16),
        pltpu.VMEM(omega.shape, BF16),
        pltpu.VMEM((RD * Y, 2 * S * Y), BF16),
        pltpu.VMEM((S // 16, R, 16 * Y), F32),
        pltpu.VMEM((R * S // Z, Z), F32),
        pltpu.VMEM((nsx, R * S // Z, Z), F32),
        pltpu.VMEM((R * S // Z, Z), F32),
        pltpu.VMEM((nsy, R * S // Z, Z), F32),
    ] + [pltpu.VMEM(E, F32)] * 7 + [
        dma((2, NC)), dma((2,)), dma((2, NC)), dma((2, NC)), dma((NC // 2,)), dma((NC // 2,)),
        dma((2, NC)), dma((2, NC)), dma((NC,)), dma((NC,)), dma((DETOUR,)), dma((DETOUR,)),
        dma((nsx,)), dma((nsx,)), dma((nsy,)), dma((nsy,)),
    ]
    any_ = pl.BlockSpec(memory_space=pl.ANY)
    hbm = pl.BlockSpec(memory_space=pltpu.HBM)
    vmem = pl.BlockSpec(memory_space=pltpu.VMEM)
    final, sketch, corange = pl.pallas_call(
        kernel,
        out_shape=(
            jax.ShapeDtypeStruct(initial_state.shape, F32),
            jax.ShapeDtypeStruct((X, RD * Y, Z), F32),
            jax.ShapeDtypeStruct(corange_prev.shape[::-1], F32),
        ),
        in_specs=[hbm, hbm, hbm, hbm],
        out_specs=(vmem, vmem, vmem),
        scratch_shapes=scratch,
        compiler_params=pltpu.CompilerParams(
            collective_id=0, has_side_effects=True, vmem_limit_bytes=VMEM_MIB * 2**20
        ),
    )(initial_state, conductivity, pltpu.with_memory_space_constraint(omega, pltpu.HBM), psi)
    final, sketch, corange = pl.pallas_call(
        store,
        out_shape=(
            jax.ShapeDtypeStruct(initial_state.shape, F32),
            jax.ShapeDtypeStruct(range_prev.shape, BF16),
            jax.ShapeDtypeStruct(corange_prev.shape[::-1], F32),
        ),
        in_specs=[vmem, vmem, vmem, vmem, vmem],
        out_specs=(any_, any_, vmem),
        scratch_shapes=[pltpu.VMEM(range_prev.shape, BF16), dma((2, PIECES))],
        compiler_params=pltpu.CompilerParams(vmem_limit_bytes=16 * 2**20),
    )(final, sketch, corange, range_prev, corange_prev.T)
    return final, sketch, corange.T


def solution(mesh):
    in_specs = (
        P("par", "sx", "sy", None),
        P("par", "sx", "sy", None),
        P(),
        P(None, "sx", "sy", None),
        P("par", "sx", "sy", None),
        P(None, "par"),
    )
    out_specs = (P("par", "sx", "sy", None), P("par", "sx", "sy", None), P(None, "par"))
    sizes = (mesh.shape["sx"], mesh.shape["sy"])
    return jax.shard_map(
        functools.partial(per_device, sizes), mesh=mesh, in_specs=in_specs, out_specs=out_specs, check_vma=False
    )
```
